512 devices in a mesh: seq: 64 (over x, z), head: 8 (over y, core).
Axes of the slice: x: 4, y: 4, z: 16, core: 2. Of those that a mesh axis runs over, the one named last changes fastest.
Arguments:
- tokens: bfloat16 [32768, 1024], P(('seq', 'head')), may hold values from -6 to 6
- w_query: bfloat16 [1024, 1024], P(None, 'head'), may hold values from -0.1875 to 0.1875
- w_key: bfloat16 [1024, 1024], P(None, 'head'), may hold values from -0.1875 to 0.1875
- w_value: bfloat16 [1024, 1024], P(None, 'head'), may hold values from -0.1875 to 0.1875
- w_beta: bfloat16 [1024, 8], P(None, 'head'), may hold values from -0.09375 to 0.09375
- beta_bias: float32 [8], P('head'), may hold values from -1 to 3, as said below
- conv_weight: float32 [3, 4, 1024], P(None, None, 'head'), may hold values from -3 to 3
- norm_gain: float32 [1024], P('head'), may hold values from 0.1 to 1.9
- w_out: bfloat16 [1024, 1024], P('head'), may hold values from -0.1875 to 0.1875
Outputs:
- mixed: bfloat16 [32768, 1024], P(('seq', 'head'))
The draws below stay inside these ranges and needn't reach their ends.
Inputs may be any that keep to these rules, and one draw needn't show every extreme that they name: `beta_bias`: one logit offset per head.
All inputs are finite; a program needn't handle non-finite values.
Results may differ from the reference program's by a relative error of at most 0.015.
The reference program's roundings to bfloat16 on the way (of `projected` and `normed`) count: a program that leaves them out, or rounds other values in their place, can miss the bound.
Values may be sent and summed in bfloat16 or wider, within the bound.
A program may use at most 64 MiB of HBM per device.

```python
import jax
import jax.numpy as jnp
from jax import lax

D = 1024
HEADS = 8
HD = 128
CONV = 4
HEADS_DEV = 1
TOKENS = 32768
N_HEAD = 8


def draw_beta_bias(key, part):
    ranking = jax.random.permutation(jax.random.fold_in(key, 11), HEADS)
    spread = jax.random.uniform(jax.random.fold_in(key, 12), (HEADS,), jnp.float32)
    keeping = ranking < HEADS // 2
    return jnp.where(keeping, 2.0 + spread, -1.0 + 2.0 * spread)


def block_scale(rng, shape, pieces, smallest, top_value):
    loudness, own = 1.0, jax.random.fold_in(rng, 6)
    for position, parts in pieces:
        draws = jnp.exp(jax.random.uniform(jax.random.fold_in(own, position), (parts,), jnp.float32, smallest / len(pieces), top_value / len(pieces)))
        loudness = loudness * jnp.repeat(draws, shape[position] // parts).reshape([-1 if axis == position else 1 for axis in range(len(shape))])
    return loudness


def scatter_about(stream_key, shape, scale, reach, pieces=(), held_as=jnp.bfloat16):
    entries = jax.random.normal(stream_key, shape, jnp.float32) * scale
    if len(pieces) > 0:
        entries = block_scale(stream_key, shape, pieces, -0.22, 0.18) * entries
    return jnp.clip(entries, min=-reach, max=reach).astype(held_as)


def setup_inputs(seed: int = 0) -> dict:
    arg_keys = jax.random.split(jax.random.key(seed), 10)
    return {
        "tokens": scatter_about(arg_keys[0], (TOKENS, D), 1.0, 6.0, ((0, 512),)),
        "w_query": scatter_about(arg_keys[1], (D, HEADS * HD), D ** -0.5, 0.1875, ((1, 8),)),
        "w_key": scatter_about(arg_keys[2], (D, HEADS * HD), D ** -0.5, 0.1875, ((1, 8),)),
        "w_value": scatter_about(arg_keys[3], (D, HEADS * HD), D ** -0.5, 0.1875, ((1, 8),)),
        "w_beta": scatter_about(arg_keys[4], (D, HEADS), (4 * D) ** -0.5, 0.09375, ((1, 8),)),
        "beta_bias": draw_beta_bias(jax.random.fold_in(arg_keys[9], 71), 0),
        "conv_weight": scatter_about(arg_keys[6], (3, CONV, HEADS * HD), CONV ** -0.5, 3.0, ((2, 8),), jnp.float32),
        "norm_gain": jnp.clip(1.0 + 0.18 * jax.random.normal(arg_keys[7], (HEADS * HD,), jnp.float32), 0.1, 1.9),
        "w_out": scatter_about(arg_keys[8], (HEADS * HD, D), (HEADS * HD) ** -0.5, 0.1875, ((0, 8),)),
    }


precise = lax.Precision.HIGHEST

def convolve(projected, weight):
    length = projected.shape[0]
    padded = jnp.concatenate([jnp.zeros((CONV - 1, projected.shape[1]), jnp.float32), projected.astype(jnp.float32)], 0)
    mixed_conv = padded[0:length] * weight[0]
    for offset in range(1, CONV):
        mixed_conv = mixed_conv + padded[offset:offset + length] * weight[offset]
    return jax.nn.silu(mixed_conv).astype(jnp.bfloat16)

def reference(tokens, w_query, w_key, w_value, w_beta, beta_bias, conv_weight, norm_gain, w_out):
    length = tokens.shape[0]
    projected = [jnp.dot(tokens, weight, preferred_element_type=jnp.float32).astype(jnp.bfloat16) for weight in (w_query, w_key, w_value)]
    queries = convolve(projected[0], conv_weight[0]).reshape(length, HEADS, HD)
    keys_raw = convolve(projected[1], conv_weight[1]).reshape(length, HEADS, HD)
    values_in = convolve(projected[2], conv_weight[2]).reshape(length, HEADS, HD)
    logits = jnp.dot(tokens, w_beta, preferred_element_type=jnp.float32) + beta_bias
    beta_rate = 2.0 * jax.nn.sigmoid(logits)
    gain_rows = norm_gain.reshape(HEADS, HD)

    def advance(carried, inputs):
        query_t, key_t, value_t, rate_t = inputs
        key_unit = key_t.astype(jnp.float32)
        key_unit = key_unit / jnp.sqrt(lax.optimization_barrier(jnp.sum(key_unit * key_unit, -1, keepdims=True)) + 1e-06)
        predicted = jnp.einsum('hvk,hk->hv', carried, key_unit, precision=precise)
        change = rate_t[:, None] * (value_t.astype(jnp.float32) - predicted)
        carried = carried + change[:, :, None] * key_unit[:, None, :]
        output = jnp.einsum('hvk,hk->hv', carried, query_t.astype(jnp.float32), precision=precise)
        scaled = output * lax.rsqrt(lax.optimization_barrier(jnp.mean(output * output, -1, keepdims=True)) + 1e-05) * gain_rows
        return (carried, scaled.astype(jnp.bfloat16))
    initial = jnp.zeros((HEADS, HD, HD), jnp.float32)
    normed = lax.scan(advance, initial, (queries, keys_raw, values_in, beta_rate))[1]
    grouped = normed.reshape(length, N_HEAD, HEADS_DEV * HD)
    weights = w_out.reshape(N_HEAD, HEADS_DEV * HD, D)
    summed = jnp.zeros((length, D), jnp.float32)
    for group_index in range(N_HEAD):
        partial_sum = jnp.dot(grouped[:, group_index], weights[group_index], preferred_element_type=jnp.float32)
        rounded = lax.optimization_barrier(partial_sum.astype(jnp.bfloat16))
        summed = summed + rounded.astype(jnp.float32)
    return summed.astype(jnp.bfloat16)
```

```python
import functools

import jax
import jax.numpy as jnp
from jax import lax
from jax.experimental import pallas as pl
from jax.experimental.pallas import tpu as pltpu
from jax.sharding import PartitionSpec as P

F32, BF16 = jnp.float32, jnp.bfloat16
MESH = pl.DeviceIdType.MESH
Z_CHIPS = 16
Y_CHIPS = 4
D = 1024
HD = 128
ROWS = 64
SHARD = 512
CHUNK = 128
CHUNKS = SHARD // CHUNK
HALF = 32
HALO = 8

NN = (((1,), (0,)), ((), ()))
NT = (((1,), (1,)), ((), ()))
TN = (((0,), (0,)), ((), ()))


def dot(a, b, dims=NN):
    return lax.dot_general(a, b, dims, preferred_element_type=F32)


def split(a):
    high = a.astype(BF16)
    return high, (a - high.astype(F32)).astype(BF16)


def mm3(a, b):
    ah, al = split(a)
    bh, bl = split(b)
    return dot(ah, bh) + (dot(ah, bl) + dot(al, bh))


def after(earlier, later):
    return mm3(earlier, later[:HD]) + pad_top(later[HD:])


def pad_top(state):
    return jnp.concatenate([jnp.zeros((HD, HD), F32), state], 0)


def prepend(raw, acc):
    high, low = split(acc[:HD])
    return dot(raw, high) + dot(raw, low) + pad_top(acc[HD:])


def append(acc, raw):
    high, low = split(acc)
    step = raw[:HD]
    return dot(high, step) + dot(low, step) + pad_top(raw[HD:].astype(F32))


def invert(lowers):
    row = lax.broadcasted_iota(jnp.int32, (CHUNK, CHUNK), 0)
    col = lax.broadcasted_iota(jnp.int32, (CHUNK, CHUNK), 1)

    def pick(low, bits):
        r, c = lax.shift_right_logical(row, bits), lax.shift_right_logical(col, bits)
        mask = (lax.bitwise_and(r, 1) == 1) & (c == r - 1)
        return jnp.where(mask, low, 0.0)

    eye = (row == col).astype(F32)
    inverses = [eye - pick(low, 0) for low in lowers]
    bits = 1
    while (1 << bits) < CHUNK:
        first = [mm3(x, pick(low, bits)) for x, low in zip(inverses, lowers)]
        inverses = [x - mm3(f, x) for x, f in zip(inverses, first)]
        bits += 1
    return inverses


def layer(
    x_chips, z_chips,
    tok, wq, wk, wv, wb, bias, conv, gain, wo,
    out,
    gathered, halo, weights, outw, padded, logits,
    q_eff, o_loc, ring, lines, left, right, total_f, entering,
    give, got,
    load_sem, tok_send, tok_recv, halo_send, halo_recv, w_send, w_recv,
    ring_send, ring_recv, line_send, line_recv, give_send, got_recv,
):
    s, h = lax.axis_index("seq"), lax.axis_index("head")
    shards = x_chips * z_chips
    y, c = h // 2, h % 2
    x, z = s // z_chips, s % z_chips
    up, down, far = (y + 1) % Y_CHIPS, (y + 3) % Y_CHIPS, (y + 2) % Y_CHIPS
    other = 1 - c
    z_up, z_down = (z + 1) % z_chips, (z + z_chips - 1) % z_chips

    def head_of(yy, cc):
        return yy * 2 + cc

    partner = (s, head_of(y, other))

    def remote(src, dst, send, recv, device):
        return pltpu.make_async_remote_copy(
            src_ref=src, dst_ref=dst, send_sem=send, recv_sem=recv,
            device_id=device, device_id_type=MESH,
        )

    def arrived(dst, recv):
        remote(dst, dst, recv, recv, partner).wait_recv()

    loads = [
        pltpu.make_async_copy(w, weights.at[:, pl.ds(i * HD, HD)], load_sem.at[i])
        for i, w in enumerate((wq, wk, wv))
    ]
    own_wo = pltpu.make_async_copy(wo, outw.at[h], load_sem.at[3])
    own_tok = [
        pltpu.make_async_copy(
            tok.at[pl.ds(i * HALF, HALF)], gathered.at[y, c, i], load_sem.at[4 + i]
        )
        for i in range(2)
    ]
    for copy in (*own_tok, *loads, own_wo):
        copy.start()

    barrier = pltpu.get_barrier_semaphore()

    def greet(device):
        pl.semaphore_signal(barrier, inc=1, device_id=device, device_id_type=MESH)

    for step in range(1, 8):
        greet((s, (h + step) % 8))
    greet((x * z_chips + z_up, h))
    greet((x * z_chips + z_down, h))
    for step in range(1, x_chips):
        greet((((x + step) % x_chips) * z_chips + z, h))

    @pl.when(s > 0)
    def _():
        greet((s - 1, 7))

    sends_halo = (h == 7) & (s < shards - 1)

    @pl.when(sends_halo)
    def _():
        for peer in range(8):
            greet((s + 1, peer))

    pl.semaphore_wait(
        barrier,
        9 + (x_chips - 1) + jnp.where(s > 0, 1, 0) + jnp.where(sends_halo, 8, 0),
    )

    sent = []

    def tok_copy(src, yy, cc, half, device):
        copy = remote(
            src, gathered.at[yy, cc, half],
            tok_send.at[len(sent)], tok_recv.at[yy, cc, half], device,
        )
        copy.start()
        sent.append(copy)

    def relay(yy, half, device):
        tok_copy(gathered.at[yy, c, half], yy, c, half, device)

    to_up, to_down = (s, head_of(up, c)), (s, head_of(down, c))
    own = [tok.at[pl.ds(i * HALF, HALF)] for i in range(2)]
    tok_copy(own[0], y, c, 0, to_up)
    tok_copy(own[1], y, c, 1, to_down)
    tok_copy(own[1], y, c, 1, to_up)
    tok_copy(own[0], y, c, 0, to_down)
    tok_copy(own[0], y, c, 0, partner)
    tok_copy(own[1], y, c, 1, partner)

    def halo_copy(peer):
        return remote(
            tok.at[pl.ds(ROWS - HALO, HALO)], halo, halo_send.at[peer], halo_recv, (s + 1, peer)
        )

    @pl.when(sends_halo)
    def _():
        for peer in range(8):
            halo_copy(peer).start()

    @pl.when(s == 0)
    def _():
        halo[...] = jnp.zeros_like(halo)

    rate_rows = jnp.broadcast_to(wb[...].astype(F32), (HD, D))
    weights[:, pl.ds(3 * HD, HD)] = jnp.transpose(rate_rows).astype(BF16)
    for copy in loads:
        copy.wait()

    def project(yy):
        block = gathered[yy].reshape(CHUNK, D)
        result = dot(block, weights[...])
        start = pl.multiple_of(yy * CHUNK, CHUNK)
        padded[pl.ds(start + HALO, CHUNK), :] = result[:, : 3 * HD].astype(BF16).astype(F32)
        logits[pl.ds(start, CHUNK), :] = result[:, 3 * HD :]

    def tok_arrived(yy, cc, half):
        arrived(gathered.at[yy, cc, half], tok_recv.at[yy, cc, half])

    tok_arrived(down, c, 0)
    relay(down, 0, to_up)
    relay(down, 0, partner)
    tok_arrived(up, c, 1)
    relay(up, 1, to_down)
    relay(up, 1, partner)
    for half in range(2):
        own_tok[half].wait()
        tok_arrived(y, other, half)
    project(y)
    tok_arrived(down, c, 1)
    relay(down, 1, partner)
    tok_arrived(up, c, 0)
    relay(up, 0, partner)

    @pl.when(s > 0)
    def _():
        arrived(halo, halo_recv)

    edge = dot(halo[...], weights[...])[:, : 3 * HD].astype(BF16).astype(F32)
    padded[pl.ds(0, HALO), :] = edge
    for yy in (down, up):
        for half in range(2):
            tok_arrived(yy, other, half)
        project(yy)
    for half in range(2):
        tok_arrived(far, c, half)
        relay(far, half, partner)
    for half in range(2):
        tok_arrived(far, other, half)
    project(far)

    own_wo.wait()
    wo_sent = []

    def wo_copy(src, slot, device):
        copy = remote(src, outw.at[slot], w_send.at[len(wo_sent)], w_recv.at[slot], device)
        copy.start()
        wo_sent.append(copy)

    wo_copy(wo, h, to_up)
    wo_copy(wo, h, to_down)
    wo_copy(wo, h, (s, head_of(far, c)))
    wo_copy(wo, h, partner)

    row = lax.broadcasted_iota(jnp.int32, (CHUNK, CHUNK), 0)
    col = lax.broadcasted_iota(jnp.int32, (CHUNK, CHUNK), 1)
    parts, lowers, rights, attends = [], [], [], []
    for n in range(CHUNKS):
        base = n * CHUNK
        acts = []
        for i in range(3):
            lanes = pl.ds(i * HD, HD)
            total = padded[pl.ds(base + HALO - 3, CHUNK), lanes] * conv[i, 0:1]
            for j in range(1, 4):
                total = total + padded[pl.ds(base + HALO - 3 + j, CHUNK), lanes] * conv[i, j : j + 1]
            acts.append((total / (1.0 + jnp.exp(-total))).astype(BF16))
        query, key, value = acts
        key32 = key.astype(F32)
        inv = 1.0 / jnp.sqrt(jnp.sum(key32 * key32, -1, keepdims=True) + 1e-06)
        beta = 2.0 * jax.nn.sigmoid(logits[pl.ds(base, CHUNK), :] + bias[...])
        rate = beta * inv
        gram = dot(key, key, NT)
        lowers.append(jnp.where(row > col, (rate * inv) * gram, 0.0))
        rights.append(
            jnp.concatenate([(rate * inv) * key32, rate * value.astype(F32)], 1)
        )
        attends.append(jnp.where(row >= col, dot(query, key, NT), 0.0).astype(BF16))
        parts.append((query, key))
    inverses = invert(lowers)
    eye = (row == col).astype(F32)
    lead = jnp.concatenate([eye, jnp.zeros((HD, HD), F32)], 0)
    before = lead
    for n in range(CHUNKS):
        query, key = parts[n]
        solved = mm3(inverses[n], rights[n])
        high, low = split(solved)
        moved = dot(high, key, TN) + dot(low, key, TN)
        step = jnp.concatenate([eye - moved[:HD], moved[HD:]], 0)
        reach = dot(attends[n], high)
        eff = (query.astype(F32) - reach[:, :HD]).astype(BF16)
        if n == 0:
            q_eff[pl.ds(0, CHUNK), :] = eff
            o_loc[pl.ds(0, CHUNK), :] = reach[:, HD:]
            before = step
        else:
            turned = dot(eff, before.astype(BF16), NT)
            q_eff[pl.ds(n * CHUNK, CHUNK), :] = turned[:, :HD].astype(BF16)
            o_loc[pl.ds(n * CHUNK, CHUNK), :] = turned[:, HD:] + reach[:, HD:]
            before = after(before, step)
    total_f[...] = before

    ring[z] = before.astype(BF16)
    ring_sent = []

    def ring_copy(slot, device_z):
        copy = remote(
            ring.at[slot], ring.at[slot],
            ring_send.at[len(ring_sent)], ring_recv.at[slot], (x * z_chips + device_z, h),
        )
        copy.start()
        ring_sent.append(copy)

    ring_copy(z, z_up)
    if z_chips > 2:
        ring_copy(z, z_down)
    for i in range(2):
        left[i] = lead
        right[i] = lead
    reach_left, reach_right = z_chips // 2, z_chips // 2 - 1
    for k in range(1, reach_left + 1):
        slot = (z + z_chips - k) % z_chips
        arrived(ring.at[slot], ring_recv.at[slot])
        if k < reach_left:
            ring_copy(slot, z_up)
        slot_r = (z + k) % z_chips
        if k <= reach_right:
            arrived(ring.at[slot_r], ring_recv.at[slot_r])
            if k < reach_right:
                ring_copy(slot_r, z_down)
        side = jnp.where(k > z, 1, 0)
        left[side] = prepend(ring[slot], left[side])
        if k <= reach_right:
            side_r = jnp.where(z + k >= z_chips, 1, 0)
            right[side_r] = append(right[side_r], ring[slot_r])
    before = after(right[1], left[0])
    line = after(before, after(total_f[...], after(right[0], left[1])))

    lines[x] = line.astype(BF16)

    def line_copy(step):
        return remote(
            lines.at[x], lines.at[x], line_send.at[step - 1], line_recv.at[x],
            ((x + step) * z_chips + z, h),
        )

    for step in range(1, x_chips):

        @pl.when(x + step < x_chips)
        def _():
            line_copy(step).start()

    entering[...] = jnp.zeros_like(entering)
    for k in range(x_chips - 1):

        @pl.when(k < x)
        def _():
            arrived(lines.at[k], line_recv.at[k])
            entering[...] = mm_state(entering[...], lines[k])

    state = mm3(entering[...], before[:HD]) + before[HD:]

    for yy in (up, down, far):
        slot = head_of(yy, c)
        arrived(outw.at[slot], w_recv.at[slot])
        wo_copy(outw.at[slot], slot, partner)

    high, low = split(state)
    outputs = dot(q_eff[...], high, NT) + dot(q_eff[...], low, NT) + o_loc[...]
    scale = lax.rsqrt(jnp.mean(outputs * outputs, -1, keepdims=True) + 1e-05)
    normed = (outputs * scale * gain[...]).astype(BF16)
    for peer in range(8):
        give[peer] = normed[peer * ROWS : (peer + 1) * ROWS]
    handed = []
    for step in range(1, 8):
        peer = (h + step) % 8
        copy = remote(
            give.at[peer], got.at[h], give_send.at[step - 1], got_recv.at[h], (s, peer)
        )
        copy.start()
        handed.append(copy)
    got[h] = give[h]
    for yy in (y, up, down, far):
        slot = head_of(yy, other)
        arrived(outw.at[slot], w_recv.at[slot])
    for step in range(1, 8):
        peer = (h + step) % 8
        arrived(got.at[peer], got_recv.at[peer])
    mixed = jnp.zeros((ROWS, D), F32)
    for g in range(8):
        mixed = mixed + dot(got[g], outw[g]).astype(BF16).astype(F32)
    out[...] = mixed.astype(BF16)

    for copy in (*sent, *wo_sent, *ring_sent, *handed):
        copy.wait_send()
    for step in range(1, x_chips):

        @pl.when(x + step < x_chips)
        def _():
            line_copy(step).wait_send()

    @pl.when(sends_halo)
    def _():
        for peer in range(8):
            halo_copy(peer).wait_send()


def mm_state(state, raw):
    high, low = split(state)
    return dot(high, raw[:HD]) + dot(low, raw[:HD]) + raw[HD:].astype(F32)


def local(x_chips, z_chips, tokens, w_query, w_key, w_value, w_beta, beta_bias, conv_weight, norm_gain, w_out):
    anywhere = pl.BlockSpec(memory_space=pl.ANY)
    vmem = pl.BlockSpec(memory_space=pltpu.VMEM)
    dma = pltpu.SemaphoreType.DMA
    return pl.pallas_call(
        functools.partial(layer, x_chips, z_chips),
        out_shape=jax.ShapeDtypeStruct((ROWS, D), BF16),
        in_specs=[anywhere] * 4 + [vmem] * 4 + [anywhere],
        out_specs=vmem,
        scratch_shapes=[
            pltpu.VMEM((Y_CHIPS, 2, 2, HALF, D), BF16),
            pltpu.VMEM((HALO, D), BF16),
            pltpu.VMEM((D, 4 * HD), BF16),
            pltpu.VMEM((8, HD, D), BF16),
            pltpu.VMEM((HALO + SHARD, 3 * HD), F32),
            pltpu.VMEM((SHARD, HD), F32),
            pltpu.VMEM((SHARD, HD), BF16),
            pltpu.VMEM((SHARD, HD), F32),
            pltpu.VMEM((z_chips, 2 * HD, HD), BF16),
            pltpu.VMEM((x_chips, 2 * HD, HD), BF16),
            pltpu.VMEM((2, 2 * HD, HD), F32),
            pltpu.VMEM((2, 2 * HD, HD), F32),
            pltpu.VMEM((2 * HD, HD), F32),
            pltpu.VMEM((HD, HD), F32),
            pltpu.VMEM((8, ROWS, HD), BF16),
            pltpu.VMEM((8, ROWS, HD), BF16),
            dma((6,)),
            dma((14,)),
            dma((Y_CHIPS, 2, 2)),
            dma((8,)),
            dma,
            dma((7,)),
            dma((8,)),
            dma((z_chips,)),
            dma((z_chips,)),
            dma((x_chips,)),
            dma((x_chips,)),
            dma((7,)),
            dma((8,)),
        ],
        compiler_params=pltpu.CompilerParams(
            collective_id=0, has_side_effects=True, vmem_limit_bytes=48 * 1024 * 1024
        ),
    )(
        tokens, w_query, w_key, w_value,
        w_beta.reshape(1, D), beta_bias.reshape(1, 1), conv_weight,
        norm_gain.reshape(1, HD), w_out,
    )


def solution(mesh):
    z_chips = Z_CHIPS
    x_chips = mesh.shape["seq"] // z_chips
    in_specs = (
        P(("seq", "head"), None),
        P(None, "head"),
        P(None, "head"),
        P(None, "head"),
        P(None, "head"),
        P("head"),
        P(None, None, "head"),
        P("head"),
        P("head", None),
    )
    out_specs = P(("seq", "head"), None)
    return jax.shard_map(
        functools.partial(local, x_chips, z_chips),
        mesh=mesh, in_specs=in_specs, out_specs=out_specs, check_vma=False,
    )
```

```python
import functools

import jax
import jax.numpy as jnp
from jax import lax
from jax.experimental import pallas as pl
from jax.experimental.pallas import tpu as pltpu
from jax.sharding import PartitionSpec as P

F32, BF16 = jnp.float32, jnp.bfloat16
MESH = pl.DeviceIdType.MESH
Z_CHIPS = 16
Y_CHIPS = 4
D = 1024
HD = 128
ROWS = 64
SHARD = 512
CHUNK = 128
CHUNKS = SHARD // CHUNK
PART = 16
HALO = 8
SUBS = 4

NN = (((1,), (0,)), ((), ()))
NT = (((1,), (1,)), ((), ()))
TN = (((0,), (0,)), ((), ()))


def dot(a, b, dims=NN):
    return lax.dot_general(a, b, dims, preferred_element_type=F32)


def split(a):
    high = a.astype(BF16)
    return high, (a - high.astype(F32)).astype(BF16)


def mm3(a, b):
    ah, al = split(a)
    bh, bl = split(b)
    return dot(ah, bh) + (dot(ah, bl) + dot(al, bh))


def after(earlier, later):
    return mm3(earlier, later[:HD]) + pad_top(later[HD:])


def pad_top(state):
    return jnp.concatenate([jnp.zeros((HD, HD), F32), state], 0)


def prepend(raw, acc):
    high, low = split(acc[:HD])
    return dot(raw, high) + dot(raw, low) + pad_top(acc[HD:])


def append(acc, raw):
    high, low = split(acc)
    step = raw[:HD]
    return dot(high, step) + dot(low, step) + pad_top(raw[HD:].astype(F32))


def invert(lowers):
    row = lax.broadcasted_iota(jnp.int32, (CHUNK, CHUNK), 0)
    col = lax.broadcasted_iota(jnp.int32, (CHUNK, CHUNK), 1)

    def pick(low, bits):
        r, c = lax.shift_right_logical(row, bits), lax.shift_right_logical(col, bits)
        mask = (lax.bitwise_and(r, 1) == 1) & (c == r - 1)
        return jnp.where(mask, low, 0.0)

    eye = (row == col).astype(F32)
    inverses = [eye - pick(low, 0) for low in lowers]
    bits = 1
    while (1 << bits) < CHUNK:
        first = [mm3(x, pick(low, bits)) for x, low in zip(inverses, lowers)]
        inverses = [x - mm3(f, x) for x, f in zip(inverses, first)]
        bits += 1
    return inverses


def layer(
    x_chips, z_chips,
    tok, wq, wk, wv, wb_in, bias_in, conv_in, gain_in, wo,
    out,
    wb, bias, conv, gain,
    gathered, halo, weights, outw, padded, logits,
    q_eff, o_loc, ring, lines, left, right, own_f, prefix, duo, entering,
    give, got,
    load_sem, tok_send, tok_recv, halo_send, halo_recv, w_send, w_recv,
    duo_send, duo_recv, ring_send, ring_recv, line_send, line_recv, give_send, got_recv,
):
    s, h = lax.axis_index("seq"), lax.axis_index("head")
    shards = x_chips * z_chips
    y, c = h // 2, h % 2
    x, z = s // z_chips, s % z_chips
    up, down, far = (y + 1) % Y_CHIPS, (y + 3) % Y_CHIPS, (y + 2) % Y_CHIPS
    other = 1 - c

    def head_of(yy, cc):
        return yy * 2 + cc

    partner = (s, head_of(y, other))

    def remote(src, dst, send, recv, device):
        return pltpu.make_async_remote_copy(
            src_ref=src, dst_ref=dst, send_sem=send, recv_sem=recv,
            device_id=device, device_id_type=MESH,
        )

    def arrived(dst, recv):
        remote(dst, dst, recv, recv, partner).wait_recv()

    loads = [
        pltpu.make_async_copy(w, weights.at[:, pl.ds(i * HD, HD)], load_sem.at[i])
        for i, w in enumerate((wq, wk, wv))
    ]
    own_wo = pltpu.make_async_copy(wo, outw.at[h], load_sem.at[3])
    small = [
        pltpu.make_async_copy(src, dst, load_sem.at[6 + i])
        for i, (src, dst) in enumerate(
            ((wb_in, wb), (bias_in, bias), (conv_in, conv), (gain_in, gain))
        )
    ]
    own_tok = [
        pltpu.make_async_copy(
            tok.at[pl.ds(i * PART, PART)], gathered.at[y, c, i], load_sem.at[10 + i]
        )
        for i in range(4)
    ]
    for copy in (*own_tok, *small, *loads, own_wo):
        copy.start()

    barrier = pltpu.get_barrier_semaphore()

    def greet(device):
        pl.semaphore_signal(barrier, inc=1, device_id=device, device_id_type=MESH)

    for step in range(1, 8):
        greet((s, (h + step) % 8))
    for hops in (z + 1 - 2 * (z % 2), (z + 2) % z_chips, (z + z_chips - 2) % z_chips):
        greet((x * z_chips + hops, h))
    for step in range(1, x_chips):
        greet((((x + step) % x_chips) * z_chips + z, h))

    @pl.when(s > 0)
    def _():
        greet((s - 1, 7))

    sends_halo = (h == 7) & (s < shards - 1)

    @pl.when(sends_halo)
    def _():
        for peer in range(8):
            greet((s + 1, peer))

    pl.semaphore_wait(
        barrier,
        10 + (x_chips - 1) + jnp.where(s > 0, 1, 0) + jnp.where(sends_halo, 8, 0),
    )

    sent = []

    def tok_copy(src, yy, cc, half, device):
        copy = remote(
            src, gathered.at[yy, cc, half],
            tok_send.at[len(sent)], tok_recv.at[yy, cc, half], device,
        )
        copy.start()
        sent.append(copy)

    def relay(yy, half, device):
        tok_copy(gathered.at[yy, c, half], yy, c, half, device)

    to_up, to_down = (s, head_of(up, c)), (s, head_of(down, c))
    for copy in own_tok:
        copy.wait()
    own = [gathered.at[y, c, i] for i in range(4)]
    for first, second in ((0, 2), (1, 3), (2, 0), (3, 1)):
        tok_copy(own[first], y, c, first, to_up)
        tok_copy(own[second], y, c, second, to_down)
    for i in range(4):
        tok_copy(own[i], y, c, i, partner)

    def halo_copy(peer):
        return remote(
            tok.at[pl.ds(ROWS - HALO, HALO)], halo, halo_send.at[peer], halo_recv, (s + 1, peer)
        )

    @pl.when(sends_halo)
    def _():
        for peer in range(8):
            halo_copy(peer).start()

    @pl.when(s == 0)
    def _():
        halo[...] = jnp.zeros_like(halo)

    for copy in small:
        copy.wait()
    rate_rows = jnp.broadcast_to(wb[...].astype(F32), (HD, D))
    weights[:, pl.ds(3 * HD, HD)] = jnp.transpose(rate_rows).astype(BF16)
    for copy in loads:
        copy.wait()

    def project(yy):
        block = gathered[yy].reshape(CHUNK, D)
        result = dot(block, weights[...])
        start = pl.multiple_of(yy * CHUNK, CHUNK)
        padded[pl.ds(start + HALO, CHUNK), :] = result[:, : 3 * HD].astype(BF16).astype(F32)
        logits[pl.ds(start, CHUNK), :] = result[:, 3 * HD :]

    def tok_arrived(yy, cc, half):
        arrived(gathered.at[yy, cc, half], tok_recv.at[yy, cc, half])

    def near_arrived(up_part, down_part, onward):
        tok_arrived(down, c, up_part)
        if onward:
            relay(down, up_part, to_up)
        relay(down, up_part, partner)
        tok_arrived(up, c, down_part)
        if onward:
            relay(up, down_part, to_down)
        relay(up, down_part, partner)

    near_arrived(0, 2, True)
    near_arrived(1, 3, True)
    for part in range(4):
        tok_arrived(y, other, part)
    project(y)
    near_arrived(2, 0, False)
    near_arrived(3, 1, False)
    @pl.when(s > 0)
    def _():
        arrived(halo, halo_recv)

    edge = dot(halo[...], weights[...])[:, : 3 * HD].astype(BF16).astype(F32)
    padded[pl.ds(0, HALO), :] = edge
    for part in (0, 2, 1, 3):
        tok_arrived(far, c, part)
        relay(far, part, partner)
    for yy in (down, up):
        for part in range(4):
            tok_arrived(yy, other, part)
        project(yy)
    for part in range(4):
        tok_arrived(far, other, part)
    project(far)

    own_wo.wait()
    wo_sent = []

    def wo_copy(src, slot, half, device):
        copy = remote(
            src.at[pl.ds(half * ROWS, ROWS)], outw.at[slot, pl.ds(half * ROWS, ROWS)],
            w_send.at[len(wo_sent)], w_recv.at[slot, half], device,
        )
        copy.start()
        wo_sent.append(copy)

    def wo_relay(yy, half, device):
        slot = head_of(yy, c)
        wo_copy(outw.at[slot], slot, half, device)

    def wo_arrived(yy, cc, half):
        slot = head_of(yy, cc)
        arrived(outw.at[slot, pl.ds(half * ROWS, ROWS)], w_recv.at[slot, half])

    wo_copy(outw.at[h], h, 0, to_up)
    wo_copy(outw.at[h], h, 1, to_down)
    wo_copy(outw.at[h], h, 1, to_up)
    wo_copy(outw.at[h], h, 0, to_down)
    wo_copy(outw.at[h], h, 0, partner)
    wo_copy(outw.at[h], h, 1, partner)

    def wo_relay_near():
        for yy, first, onward in ((down, 0, to_up), (up, 1, to_down)):
            wo_arrived(yy, c, first)
            wo_relay(yy, first, onward)
        for yy in (down, up):
            for half in range(2):
                if (yy is down) == (half == 1):
                    wo_arrived(yy, c, half)
                wo_relay(yy, half, partner)

    def wo_relay_far():
        for half in range(2):
            wo_arrived(far, c, half)
            wo_relay(far, half, partner)

    row = lax.broadcasted_iota(jnp.int32, (CHUNK, CHUNK), 0)
    col = lax.broadcasted_iota(jnp.int32, (CHUNK, CHUNK), 1)
    parts, lowers, rights, attends = [], [], [], []
    for n in range(CHUNKS):
        base = n * CHUNK
        acts = []
        for i in range(3):
            lanes = pl.ds(i * HD, HD)
            total = padded[pl.ds(base + HALO - 3, CHUNK), lanes] * conv[i, 0:1]
            for j in range(1, 4):
                total = total + padded[pl.ds(base + HALO - 3 + j, CHUNK), lanes] * conv[i, j : j + 1]
            acts.append((total / (1.0 + jnp.exp(-total))).astype(BF16))
        query, key, value = acts
        key32 = key.astype(F32)
        inv = 1.0 / jnp.sqrt(jnp.sum(key32 * key32, -1, keepdims=True) + 1e-06)
        beta = 2.0 * jax.nn.sigmoid(logits[pl.ds(base, CHUNK), :] + bias[0])
        rate = beta * inv
        gram = dot(key, key, NT)
        lowers.append(jnp.where(row > col, (rate * inv) * gram, 0.0))
        rights.append(
            jnp.concatenate([(rate * inv) * key32, rate * value.astype(F32)], 1)
        )
        attends.append(jnp.where(row >= col, dot(query, key, NT), 0.0).astype(BF16))
        parts.append((query, key))
    inverses = invert(lowers)
    eye = (row == col).astype(F32)
    lead = jnp.concatenate([eye, jnp.zeros((HD, HD), F32)], 0)
    before, entry, reached = lead, [], []
    for n in range(CHUNKS):
        query, key = parts[n]
        solved = mm3(inverses[n], rights[n])
        high, low = split(solved)
        moved = dot(high, key, TN) + dot(low, key, TN)
        step = jnp.concatenate([eye - moved[:HD], moved[HD:]], 0)
        entry.append(before)
        reached.append(high)
        before = step if n == 0 else after(before, step)

    def finish_outputs():
        for n in range(CHUNKS):
            reach = dot(attends[n], reached[n])
            eff = (parts[n][0].astype(F32) - reach[:, :HD]).astype(BF16)
            if n == 0:
                q_eff[pl.ds(0, CHUNK), :] = eff
                o_loc[pl.ds(0, CHUNK), :] = reach[:, HD:]
            else:
                turned = dot(eff, entry[n].astype(BF16), NT)
                q_eff[pl.ds(n * CHUNK, CHUNK), :] = turned[:, :HD].astype(BF16)
                o_loc[pl.ds(n * CHUNK, CHUNK), :] = turned[:, HD:] + reach[:, HD:]


    halves = z % 2
    z_other = z + 1 - 2 * halves
    duo[halves] = before.astype(BF16)
    duo_copy = remote(
        duo.at[halves], duo.at[halves], duo_send, duo_recv.at[halves], (x * z_chips + z_other, h)
    )
    duo_copy.start()
    finish_outputs()
    for i in range(2):
        left[i] = lead
        right[i] = lead
    arrived(duo.at[1 - halves], duo_recv.at[1 - halves])

    @pl.when(halves == 0)
    def _():
        own_f[...] = append(before, duo[1])

    @pl.when(halves == 1)
    def _():
        own_f[...] = prepend(duo[0], before)

    pairs = z_chips // 2
    j = z // 2
    ring[j] = own_f[...].astype(BF16).reshape(SUBS, 2 * HD // SUBS, HD)
    ring_sent = []
    two_up = (x * z_chips + (z + 2) % z_chips, h)
    two_down = (x * z_chips + (z + z_chips - 2) % z_chips, h)

    def ring_copy(slot, q, device):
        copy = remote(
            ring.at[slot, q], ring.at[slot, q],
            ring_send.at[len(ring_sent)], ring_recv.at[slot, q], device,
        )
        copy.start()
        ring_sent.append(copy)

    reach_left, reach_right = pairs // 2, (pairs - 1) // 2
    for q in range(SUBS):
        ring_copy(j, q, two_up)
        if reach_right > 0:
            ring_copy(j, q, two_down)

    def compose(k):
        slot = (j + pairs - k) % pairs
        side = jnp.where(k > j, 1, 0)
        left[side] = prepend(ring[slot].reshape(2 * HD, HD), left[side])
        if k <= reach_right:
            slot_r = (j + k) % pairs
            side_r = jnp.where(j + k >= pairs, 1, 0)
            right[side_r] = append(right[side_r], ring[slot_r].reshape(2 * HD, HD))

    for k in range(1, reach_left + 1):
        slot = (j + pairs - k) % pairs
        slot_r = (j + k) % pairs
        for q in range(SUBS):
            arrived(ring.at[slot, q], ring_recv.at[slot, q])
            if k < reach_left:
                ring_copy(slot, q, two_up)
            if k <= reach_right:
                arrived(ring.at[slot_r, q], ring_recv.at[slot_r, q])
                if k < reach_right:
                    ring_copy(slot_r, q, two_down)
        if k == 1:
            wo_relay_near()
        if k == max(1, reach_left - 1):
            wo_relay_far()
            for done in range(1, k + 1):
                compose(done)
    if reach_left > 1:
        compose(reach_left)
    before = after(right[1], left[0])
    line = after(before, after(own_f[...], after(right[0], left[1])))
    prefix[...] = before

    @pl.when(halves == 1)
    def _():
        prefix[...] = append(before, duo[0])

    lines[x] = line.astype(BF16)

    def line_copy(step):
        return remote(
            lines.at[x], lines.at[x], line_send.at[step - 1], line_recv.at[x],
            ((x + step) * z_chips + z, h),
        )

    for step in range(1, x_chips):

        @pl.when(x + step < x_chips)
        def _():
            line_copy(step).start()

    entering[...] = jnp.zeros_like(entering)
    for k in range(x_chips - 1):

        @pl.when(k < x)
        def _():
            arrived(lines.at[k], line_recv.at[k])
            entering[...] = mm_state(entering[...], lines[k])

    state = mm3(entering[...], prefix[pl.ds(0, HD)]) + prefix[pl.ds(HD, HD)]

    high, low = split(state)
    outputs = dot(q_eff[...], high, NT) + dot(q_eff[...], low, NT) + o_loc[...]
    scale = lax.rsqrt(jnp.mean(outputs * outputs, -1, keepdims=True) + 1e-05)
    normed = (outputs * scale * gain[...]).astype(BF16)
    for peer in range(8):
        give[peer] = normed[peer * ROWS : (peer + 1) * ROWS]
    handed = []
    for step in range(1, 8):
        peer = (h + step) % 8
        copy = remote(
            give.at[peer], got.at[h], give_send.at[step - 1], got_recv.at[h], (s, peer)
        )
        copy.start()
        handed.append(copy)
    got[h] = give[h]
    for yy in (y, up, down, far):
        for half in range(2):
            wo_arrived(yy, other, half)
    for step in range(1, 8):
        peer = (h + step) % 8
        arrived(got.at[peer], got_recv.at[peer])
    mixed = jnp.zeros((ROWS, D), F32)
    for g in range(8):
        mixed = mixed + dot(got[g], outw[g]).astype(BF16).astype(F32)
    out[...] = mixed.astype(BF16)

    for copy in (*sent, *wo_sent, duo_copy, *ring_sent, *handed):
        copy.wait_send()
    for step in range(1, x_chips):

        @pl.when(x + step < x_chips)
        def _():
            line_copy(step).wait_send()

    @pl.when(sends_halo)
    def _():
        for peer in range(8):
            halo_copy(peer).wait_send()


def mm_state(state, raw):
    high, low = split(state)
    return dot(high, raw[:HD]) + dot(low, raw[:HD]) + raw[HD:].astype(F32)


def local(x_chips, z_chips, tokens, w_query, w_key, w_value, w_beta, beta_bias, conv_weight, norm_gain, w_out):
    hbm = pl.BlockSpec(memory_space=pltpu.HBM)
    vmem = pl.BlockSpec(memory_space=pltpu.VMEM)
    dma = pltpu.SemaphoreType.DMA
    return pl.pallas_call(
        functools.partial(layer, x_chips, z_chips),
        out_shape=jax.ShapeDtypeStruct((ROWS, D), BF16),
        in_specs=[hbm] * 9,
        out_specs=vmem,
        scratch_shapes=[
            pltpu.VMEM((1, D), BF16),
            pltpu.SMEM((1,), F32),
            pltpu.VMEM((3, 4, HD), F32),
            pltpu.VMEM((1, HD), F32),
            pltpu.VMEM((Y_CHIPS, 2, 4, PART, D), BF16),
            pltpu.VMEM((HALO, D), BF16),
            pltpu.VMEM((D, 4 * HD), BF16),
            pltpu.VMEM((8, HD, D), BF16),
            pltpu.VMEM((HALO + SHARD, 3 * HD), F32),
            pltpu.VMEM((SHARD, HD), F32),
            pltpu.VMEM((SHARD, HD), BF16),
            pltpu.VMEM((SHARD, HD), F32),
            pltpu.VMEM((z_chips // 2, SUBS, 2 * HD // SUBS, HD), BF16),
            pltpu.VMEM((x_chips, 2 * HD, HD), BF16),
            pltpu.VMEM((2, 2 * HD, HD), F32),
            pltpu.VMEM((2, 2 * HD, HD), F32),
            pltpu.VMEM((2 * HD, HD), F32),
            pltpu.VMEM((2 * HD, HD), F32),
            pltpu.VMEM((2, 2 * HD, HD), BF16),
            pltpu.VMEM((HD, HD), F32),
            pltpu.VMEM((8, ROWS, HD), BF16),
            pltpu.VMEM((8, ROWS, HD), BF16),
            dma((14,)),
            dma((28,)),
            dma((Y_CHIPS, 2, 4)),
            dma((8,)),
            dma,
            dma((14,)),
            dma((8, 2)),
            dma,
            dma((2,)),
            dma((z_chips // 2 * SUBS,)),
            dma((z_chips // 2, SUBS)),
            dma((x_chips,)),
            dma((x_chips,)),
            dma((7,)),
            dma((8,)),
        ],
        compiler_params=pltpu.CompilerParams(
            collective_id=0, has_side_effects=True, vmem_limit_bytes=67043328
        ),
    )(
        tokens, w_query, w_key, w_value,
        w_beta.reshape(1, D), beta_bias, conv_weight,
        norm_gain.reshape(1, HD), w_out,
    )


def solution(mesh):
    z_chips = Z_CHIPS
    x_chips = mesh.shape["seq"] // z_chips
    in_specs = (
        P(("seq", "head"), None),
        P(None, "head"),
        P(None, "head"),
        P(None, "head"),
        P(None, "head"),
        P("head"),
        P(None, None, "head"),
        P("head"),
        P("head", None),
    )
    out_specs = P(("seq", "head"), None)
    return jax.shard_map(
        functools.partial(local, x_chips, z_chips),
        mesh=mesh, in_specs=in_specs, out_specs=out_specs, check_vma=False,
    )
```

```python
import functools

import jax
import jax.numpy as jnp
from jax import lax
from jax.experimental import pallas as pl
from jax.experimental.pallas import tpu as pltpu
from jax.sharding import PartitionSpec as P

F32, BF16 = jnp.float32, jnp.bfloat16
MESH = pl.DeviceIdType.MESH
Z_CHIPS = 16
Y_CHIPS = 4
D = 1024
HD = 128
ROWS = 64
SHARD = 512
CHUNK = 128
CHUNKS = SHARD // CHUNK
PART = 16
HALO = 8
SUBS = 4
RING_SENDS = {2: 1, 8: 7}

NN = (((1,), (0,)), ((), ()))
NT = (((1,), (1,)), ((), ()))
TN = (((0,), (0,)), ((), ()))


def dot(a, b, dims=NN):
    return lax.dot_general(a, b, dims, preferred_element_type=F32)


def split(a):
    high = a.astype(BF16)
    return high, (a - high.astype(F32)).astype(BF16)


def mm3(a, b):
    ah, al = split(a)
    bh, bl = split(b)
    return dot(ah, bh) + (dot(ah, bl) + dot(al, bh))


def after(earlier, later):
    return mm3(earlier, later[:HD]) + pad_top(later[HD:])


def pad_top(state):
    return jnp.concatenate([jnp.zeros((HD, HD), F32), state], 0)


def prepend(raw, acc):
    high, low = split(acc[:HD])
    return dot(raw, high) + dot(raw, low) + pad_top(acc[HD:])


def append(acc, raw):
    high, low = split(acc)
    step = raw[:HD]
    return dot(high, step) + dot(low, step) + pad_top(raw[HD:].astype(F32))


def invert(lowers):
    row = lax.broadcasted_iota(jnp.int32, (CHUNK, CHUNK), 0)
    col = lax.broadcasted_iota(jnp.int32, (CHUNK, CHUNK), 1)

    def pick(low, bits):
        r, c = lax.shift_right_logical(row, bits), lax.shift_right_logical(col, bits)
        mask = (lax.bitwise_and(r, 1) == 1) & (c == r - 1)
        return jnp.where(mask, low, 0.0)

    eye = (row == col).astype(F32)
    inverses = [eye - pick(low, 0) for low in lowers]
    bits = 1
    while (1 << bits) < CHUNK:
        first = [mm3(x, pick(low, bits)) for x, low in zip(inverses, lowers)]
        inverses = [x - mm3(f, x) for x, f in zip(inverses, first)]
        bits += 1
    return inverses


def layer(
    x_chips, z_chips,
    tok, wq, wk, wv, wb_in, bias_in, conv_in, gain_in, wo,
    out,
    wb, bias, conv, gain,
    gathered, halo, weights, outw, padded, logits,
    q_eff, o_loc, ring, lines, left, right, own_f, prefix, duo, entering,
    give, got,
    load_sem, tok_send, tok_recv, halo_send, halo_recv, w_send, w_recv,
    duo_send, duo_recv, ring_send, ring_recv, line_send, line_recv, give_send, got_recv,
):
    s, h = lax.axis_index("seq"), lax.axis_index("head")
    shards = x_chips * z_chips
    y, c = h // 2, h % 2
    x, z = s // z_chips, s % z_chips
    up, down, far = (y + 1) % Y_CHIPS, (y + 3) % Y_CHIPS, (y + 2) % Y_CHIPS
    other = 1 - c

    def head_of(yy, cc):
        return yy * 2 + cc

    partner = (s, head_of(y, other))

    def remote(src, dst, send, recv, device):
        return pltpu.make_async_remote_copy(
            src_ref=src, dst_ref=dst, send_sem=send, recv_sem=recv,
            device_id=device, device_id_type=MESH,
        )

    def arrived(dst, recv):
        remote(dst, dst, recv, recv, partner).wait_recv()

    def settle(shape_of, sem):
        pltpu.make_async_copy(shape_of, shape_of, sem).wait()

    loads = [
        pltpu.make_async_copy(w, weights.at[:, pl.ds(i * HD, HD)], load_sem.at[0])
        for i, w in enumerate((wq, wk, wv))
    ]
    own_wo = pltpu.make_async_copy(wo, outw.at[h], load_sem.at[1])
    small = [
        pltpu.make_async_copy(src, dst, load_sem.at[3 + i])
        for i, (src, dst) in enumerate(
            ((wb_in, wb), (bias_in, bias), (conv_in, conv), (gain_in, gain))
        )
    ]
    own_tok = [
        pltpu.make_async_copy(
            tok.at[pl.ds(i * PART, PART)], gathered.at[y, c, i], load_sem.at[2]
        )
        for i in range(4)
    ]
    for copy in (*own_tok, *small, *loads, own_wo):
        copy.start()

    barrier = pltpu.get_barrier_semaphore()

    def greet(device):
        pl.semaphore_signal(barrier, inc=1, device_id=device, device_id_type=MESH)

    for step in range(1, 8):
        greet((s, (h + step) % 8))
    for hops in (z + 1 - 2 * (z % 2), (z + 2) % z_chips, (z + z_chips - 2) % z_chips):
        greet((x * z_chips + hops, h))
    for step in range(1, x_chips):
        greet((((x + step) % x_chips) * z_chips + z, h))

    @pl.when(s > 0)
    def _():
        greet((s - 1, 7))

    sends_halo = (h == 7) & (s < shards - 1)

    @pl.when(sends_halo)
    def _():
        for peer in range(8):
            greet((s + 1, peer))

    pl.semaphore_wait(
        barrier,
        10 + (x_chips - 1) + jnp.where(s > 0, 1, 0) + jnp.where(sends_halo, 8, 0),
    )

    def tok_copy(src, yy, cc, part, device, kind):
        recv = tok_recv.at[yy, 4] if device is partner else tok_recv.at[yy, part]
        remote(src, gathered.at[yy, cc, part], tok_send.at[kind], recv, device).start()

    def relay(yy, half, device):
        tok_copy(gathered.at[yy, c, half], yy, c, half, device, 1)

    to_up, to_down = (s, head_of(up, c)), (s, head_of(down, c))
    settle(gathered.at[y, c], load_sem.at[2])
    own = [gathered.at[y, c, i] for i in range(4)]
    for first, second in ((0, 2), (1, 3), (2, 0), (3, 1)):
        tok_copy(own[first], y, c, first, to_up, 0)
        tok_copy(own[second], y, c, second, to_down, 0)
    for i in range(4):
        tok_copy(own[i], y, c, i, partner, 0)

    def halo_copy(peer):
        return remote(
            tok.at[pl.ds(ROWS - HALO, HALO)], halo, halo_send, halo_recv, (s + 1, peer)
        )

    @pl.when(sends_halo)
    def _():
        for peer in range(8):
            halo_copy(peer).start()

    @pl.when(s == 0)
    def _():
        halo[...] = jnp.zeros_like(halo)

    for copy in small:
        copy.wait()
    rate_rows = jnp.broadcast_to(wb[...].astype(F32), (HD, D))
    weights[:, pl.ds(3 * HD, HD)] = jnp.transpose(rate_rows).astype(BF16)
    settle(weights.at[:, pl.ds(0, 3 * HD)], load_sem.at[0])

    def project(yy):
        block = gathered[yy].reshape(CHUNK, D)
        result = dot(block, weights[...])
        start = pl.multiple_of(yy * CHUNK, CHUNK)
        padded[pl.ds(start + HALO, CHUNK), :] = result[:, : 3 * HD].astype(BF16).astype(F32)
        logits[pl.ds(start, CHUNK), :] = result[:, 3 * HD :]

    def tok_arrived(yy, part):
        arrived(gathered.at[yy, c, part], tok_recv.at[yy, part])

    def tok_other_arrived(yy):
        arrived(gathered.at[yy, other], tok_recv.at[yy, 4])

    def near_arrived(up_part, down_part, onward):
        tok_arrived(down, up_part)
        if onward:
            relay(down, up_part, to_up)
        relay(down, up_part, partner)
        tok_arrived(up, down_part)
        if onward:
            relay(up, down_part, to_down)
        relay(up, down_part, partner)

    near_arrived(0, 2, True)
    near_arrived(1, 3, True)
    tok_other_arrived(y)
    project(y)
    near_arrived(2, 0, False)
    near_arrived(3, 1, False)
    @pl.when(s > 0)
    def _():
        arrived(halo, halo_recv)

    edge = dot(halo[...], weights[...])[:, : 3 * HD].astype(BF16).astype(F32)
    padded[pl.ds(0, HALO), :] = edge
    for part in (0, 2, 1, 3):
        tok_arrived(far, part)
        relay(far, part, partner)
    for yy in (down, up):
        tok_other_arrived(yy)
        project(yy)
    tok_other_arrived(far)
    project(far)

    own_wo.wait()

    def wo_copy(src, slot, half, device):
        rows = pl.ds(half * ROWS, ROWS)
        recv = w_recv.at[slot // 2, 2 if device is partner else half]
        remote(src.at[rows], outw.at[slot, rows], w_send, recv, device).start()

    def wo_relay(yy, half, device):
        slot = head_of(yy, c)
        wo_copy(outw.at[slot], slot, half, device)

    def wo_arrived(yy, half):
        slot = head_of(yy, c)
        arrived(outw.at[slot, pl.ds(half * ROWS, ROWS)], w_recv.at[yy, half])

    wo_copy(outw.at[h], h, 0, to_up)
    wo_copy(outw.at[h], h, 1, to_down)
    wo_copy(outw.at[h], h, 1, to_up)
    wo_copy(outw.at[h], h, 0, to_down)
    wo_copy(outw.at[h], h, 0, partner)
    wo_copy(outw.at[h], h, 1, partner)

    def wo_relay_near():
        for yy, first, onward in ((down, 0, to_up), (up, 1, to_down)):
            wo_arrived(yy, first)
            wo_relay(yy, first, onward)
        for yy in (down, up):
            for half in range(2):
                if (yy is down) == (half == 1):
                    wo_arrived(yy, half)
                wo_relay(yy, half, partner)

    def wo_relay_far():
        for half in range(2):
            wo_arrived(far, half)
            wo_relay(far, half, partner)

    row = lax.broadcasted_iota(jnp.int32, (CHUNK, CHUNK), 0)
    col = lax.broadcasted_iota(jnp.int32, (CHUNK, CHUNK), 1)
    parts, lowers, rights, attends = [], [], [], []
    for n in range(CHUNKS):
        base = n * CHUNK
        acts = []
        for i in range(3):
            lanes = pl.ds(i * HD, HD)
            total = padded[pl.ds(base + HALO - 3, CHUNK), lanes] * conv[i, 0:1]
            for j in range(1, 4):
                total = total + padded[pl.ds(base + HALO - 3 + j, CHUNK), lanes] * conv[i, j : j + 1]
            acts.append((total / (1.0 + jnp.exp(-total))).astype(BF16))
        query, key, value = acts
        key32 = key.astype(F32)
        inv = 1.0 / jnp.sqrt(jnp.sum(key32 * key32, -1, keepdims=True) + 1e-06)
        beta = 2.0 * jax.nn.sigmoid(logits[pl.ds(base, CHUNK), :] + bias[0])
        rate = beta * inv
        gram = dot(key, key, NT)
        lowers.append(jnp.where(row > col, (rate * inv) * gram, 0.0))
        rights.append(
            jnp.concatenate([(rate * inv) * key32, rate * value.astype(F32)], 1)
        )
        attends.append(jnp.where(row >= col, dot(query, key, NT), 0.0).astype(BF16))
        parts.append((query, key))
    inverses = invert(lowers)
    eye = (row == col).astype(F32)
    lead = jnp.concatenate([eye, jnp.zeros((HD, HD), F32)], 0)
    before, entry, reached = lead, [], []
    for n in range(CHUNKS):
        query, key = parts[n]
        solved = mm3(inverses[n], rights[n])
        high, low = split(solved)
        moved = dot(high, key, TN) + dot(low, key, TN)
        step = jnp.concatenate([eye - moved[:HD], moved[HD:]], 0)
        entry.append(before)
        reached.append(high)
        before = step if n == 0 else after(before, step)

    def finish_outputs():
        for n in range(CHUNKS):
            reach = dot(attends[n], reached[n])
            eff = (parts[n][0].astype(F32) - reach[:, :HD]).astype(BF16)
            if n == 0:
                q_eff[pl.ds(0, CHUNK), :] = eff
                o_loc[pl.ds(0, CHUNK), :] = reach[:, HD:]
            else:
                turned = dot(eff, entry[n].astype(BF16), NT)
                q_eff[pl.ds(n * CHUNK, CHUNK), :] = turned[:, :HD].astype(BF16)
                o_loc[pl.ds(n * CHUNK, CHUNK), :] = turned[:, HD:] + reach[:, HD:]


    halves = z % 2
    z_other = z + 1 - 2 * halves
    duo[halves] = before.astype(BF16)
    duo_copy = remote(
        duo.at[halves], duo.at[halves], duo_send, duo_recv.at[halves], (x * z_chips + z_other, h)
    )
    duo_copy.start()
    finish_outputs()
    for i in range(2):
        left[i] = lead
        right[i] = lead
    arrived(duo.at[1 - halves], duo_recv.at[1 - halves])

    @pl.when(halves == 0)
    def _():
        own_f[...] = append(before, duo[1])

    @pl.when(halves == 1)
    def _():
        own_f[...] = prepend(duo[0], before)

    pairs = z_chips // 2
    j = z // 2
    ring[j] = own_f[...].astype(BF16).reshape(SUBS, 2 * HD // SUBS, HD)
    two_up = (x * z_chips + (z + 2) % z_chips, h)
    two_down = (x * z_chips + (z + z_chips - 2) % z_chips, h)

    def ring_copy(slot, q, device):
        remote(
            ring.at[slot, q], ring.at[slot, q], ring_send, ring_recv.at[slot, q], device
        ).start()

    reach = pairs // 2

    def ring_pass(slot, q, step):
        if step < reach or (step == reach and q < SUBS // 2):
            ring_copy(slot, q, two_up)

    def ring_pass_down(slot, q, step):
        if step < reach or (step == reach and q >= SUBS // 2):
            ring_copy(slot, q, two_down)

    for q in range(SUBS):
        ring_pass(j, q, 1)
        ring_pass_down(j, q, 1)

    def compose(k):
        slot = (j + pairs - k) % pairs
        side = jnp.where(k > j, 1, 0)
        left[side] = prepend(ring[slot].reshape(2 * HD, HD), left[side])
        if k < reach:
            slot_r = (j + k) % pairs
            side_r = jnp.where(j + k >= pairs, 1, 0)
            right[side_r] = append(right[side_r], ring[slot_r].reshape(2 * HD, HD))

    for k in range(1, reach + 1):
        slot = (j + pairs - k) % pairs
        slot_r = (j + k) % pairs
        for q in range(SUBS):
            if k < reach or q < SUBS // 2:
                arrived(ring.at[slot, q], ring_recv.at[slot, q])
                ring_pass(slot, q, k + 1)
            if k < reach or q >= SUBS // 2:
                arrived(ring.at[slot_r, q], ring_recv.at[slot_r, q])
                ring_pass_down(slot_r, q, k + 1)
        if k == 1:
            wo_relay_near()
        if k == max(1, reach - 1):
            wo_relay_far()
            for done in range(1, k + 1):
                compose(done)
    if reach > 1:
        compose(reach)
    before = after(right[1], left[0])
    line = after(before, after(own_f[...], after(right[0], left[1])))
    prefix[...] = before

    @pl.when(halves == 1)
    def _():
        prefix[...] = append(before, duo[0])

    lines[x] = line.astype(BF16).reshape(2, HD, HD)
    moves = [
        (0, 1, 0, 1), (0, 3, 0, 1), (0, 2, 0, 1), (1, 3, 1, 0), (1, 2, 1, 0),
        (1, 2, 1, 1), (1, 0, 1, 1), (2, 3, 2, 0), (2, 3, 2, 1), (0, 3, 1, 1),
    ]

    def line_copy(i):
        _, to, slot, part = moves[i]
        return remote(
            lines.at[slot, part], lines.at[slot, part], line_send,
            line_recv.at[slot, part], (to * z_chips + z, h),
        )

    def line_arrived(slot, part):
        arrived(lines.at[slot, part], line_recv.at[slot, part])

    if x_chips == 4:
        for i, move in enumerate(moves):

            @pl.when(x == move[0])
            def _():
                if i == len(moves) - 1:
                    line_arrived(1, 1)
                line_copy(i).start()

    entering[...] = jnp.zeros_like(entering)
    for k in range(x_chips - 1):

        @pl.when(k < x)
        def _():
            line_arrived(k, 1)
            if k == 0:
                entering[...] = lines[0, 1].astype(F32)
            else:
                line_arrived(k, 0)
                high, low = split(entering[...])
                step = lines[k, 0]
                entering[...] = dot(high, step) + dot(low, step) + lines[k, 1].astype(F32)

    state = mm3(entering[...], prefix[pl.ds(0, HD)]) + prefix[pl.ds(HD, HD)]

    high, low = split(state)
    outputs = dot(q_eff[...], high, NT) + dot(q_eff[...], low, NT) + o_loc[...]
    scale = lax.rsqrt(jnp.mean(outputs * outputs, -1, keepdims=True) + 1e-05)
    normed = (outputs * scale * gain[...]).astype(BF16)
    for peer in range(8):
        give[peer] = normed[peer * ROWS : (peer + 1) * ROWS]
    order = [head_of(yy, cc) for yy, cc in (
        (far, c), (far, other), (up, c), (down, c), (up, other), (down, other), (y, other)
    )]
    for peer in order:
        remote(give.at[peer], got.at[h], give_send, got_recv, (s, peer)).start()
    got[h] = give[h]
    for yy in (y, up, down, far):
        arrived(outw.at[head_of(yy, other)], w_recv.at[yy, 2])
    settle(got.at[pl.ds(0, 7)], got_recv)
    mixed = jnp.zeros((ROWS, D), F32)
    for g in range(8):
        mixed = mixed + dot(got[g], outw[g]).astype(BF16).astype(F32)
    out[...] = mixed.astype(BF16)

    settle(gathered.at[pl.ds(0, 3), 0], tok_send.at[0])
    settle(gathered.at[:, 0], tok_send.at[1])
    settle(outw.at[pl.ds(0, 7)], w_send)
    settle(ring.at[pl.ds(0, RING_SENDS[pairs])], ring_send)
    settle(give.at[pl.ds(0, 7)], give_send)
    duo_copy.wait_send()
    if x_chips == 4:

        @pl.when(x < 2)
        def _():
            settle(lines.at[pl.ds(0, 2)], line_send)

        @pl.when(x == 2)
        def _():
            settle(lines.at[0], line_send)

    @pl.when(sends_halo)
    def _():
        settle(gathered.at[0, 0], halo_send)


def local(x_chips, z_chips, tokens, w_query, w_key, w_value, w_beta, beta_bias, conv_weight, norm_gain, w_out):
    hbm = pl.BlockSpec(memory_space=pltpu.HBM)
    vmem = pl.BlockSpec(memory_space=pltpu.VMEM)
    dma = pltpu.SemaphoreType.DMA
    return pl.pallas_call(
        functools.partial(layer, x_chips, z_chips),
        out_shape=jax.ShapeDtypeStruct((ROWS, D), BF16),
        in_specs=[hbm] * 9,
        out_specs=vmem,
        scratch_shapes=[
            pltpu.VMEM((1, D), BF16),
            pltpu.SMEM((1,), F32),
            pltpu.VMEM((3, 4, HD), F32),
            pltpu.VMEM((1, HD), F32),
            pltpu.VMEM((Y_CHIPS, 2, 4, PART, D), BF16),
            pltpu.VMEM((HALO, D), BF16),
            pltpu.VMEM((D, 4 * HD), BF16),
            pltpu.VMEM((8, HD, D), BF16),
            pltpu.VMEM((HALO + SHARD, 3 * HD), F32),
            pltpu.VMEM((SHARD, HD), F32),
            pltpu.VMEM((SHARD, HD), BF16),
            pltpu.VMEM((SHARD, HD), F32),
            pltpu.VMEM((z_chips // 2, SUBS, 2 * HD // SUBS, HD), BF16),
            pltpu.VMEM((x_chips, 2, HD, HD), BF16),
            pltpu.VMEM((2, 2 * HD, HD), F32),
            pltpu.VMEM((2, 2 * HD, HD), F32),
            pltpu.VMEM((2 * HD, HD), F32),
            pltpu.VMEM((2 * HD, HD), F32),
            pltpu.VMEM((2, 2 * HD, HD), BF16),
            pltpu.VMEM((HD, HD), F32),
            pltpu.VMEM((8, ROWS, HD), BF16),
            pltpu.VMEM((8, ROWS, HD), BF16),
            dma((7,)),
            dma((2,)),
            dma((Y_CHIPS, 5)),
            dma,
            dma,
            dma,
            dma((Y_CHIPS, 3)),
            dma,
            dma((2,)),
            dma,
            dma((z_chips // 2, SUBS)),
            dma,
            dma((x_chips, 2)),
            dma,
            dma,
        ],
        compiler_params=pltpu.CompilerParams(
            collective_id=0, has_side_effects=True, vmem_limit_bytes=48 * 1024 * 1024
        ),
    )(
        keep(tokens), keep(w_query), keep(w_key), keep(w_value),
        keep(w_beta.reshape(1, D)), beta_bias, keep(conv_weight),
        keep(norm_gain.reshape(1, HD)), keep(w_out),
    )


def keep(a):
    return pltpu.with_memory_space_constraint(a, pltpu.HBM)


def solution(mesh):
    z_chips = Z_CHIPS
    x_chips = mesh.shape["seq"] // z_chips
    in_specs = (
        P(("seq", "head"), None),
        P(None, "head"),
        P(None, "head"),
        P(None, "head"),
        P(None, "head"),
        P("head"),
        P(None, None, "head"),
        P("head"),
        P("head", None),
    )
    out_specs = P(("seq", "head"), None)
    return jax.shard_map(
        functools.partial(local, x_chips, z_chips),
        mesh=mesh, in_specs=in_specs, out_specs=out_specs, check_vma=False,
    )
```

```python
import functools

import jax
import jax.numpy as jnp
from jax import lax
from jax.experimental import pallas as pl
from jax.experimental.pallas import tpu as pltpu
from jax.sharding import PartitionSpec as P

F32, BF16 = jnp.float32, jnp.bfloat16
MESH = pl.DeviceIdType.MESH
Z_CHIPS = 16
Y_CHIPS = 4
D = 1024
HD = 128
ROWS = 64
SHARD = 512
CHUNK = 128
CHUNKS = SHARD // CHUNK
PART = 16
HALO = 8
SUBS = 4
HALF_SUBS = SUBS // 2
RING_SENDS = {2: 1, 8: 7}

NN = (((1,), (0,)), ((), ()))
NT = (((1,), (1,)), ((), ()))
TN = (((0,), (0,)), ((), ()))


def dot(a, b, dims=NN):
    return lax.dot_general(a, b, dims, preferred_element_type=F32)


def split(a):
    high = a.astype(BF16)
    return high, (a - high.astype(F32)).astype(BF16)


def mm3(a, b):
    ah, al = split(a)
    bh, bl = split(b)
    return dot(ah, bh) + (dot(ah, bl) + dot(al, bh))


def after(earlier, later):
    return mm3(earlier, later[:HD]) + pad_top(later[HD:])


def pad_top(state):
    return jnp.concatenate([jnp.zeros((HD, HD), F32), state], 0)


def prepend(raw, acc):
    high, low = split(acc[:HD])
    return dot(raw, high) + dot(raw, low) + pad_top(acc[HD:])


def append(acc, raw):
    high, low = split(acc)
    step = raw[:HD]
    return dot(high, step) + dot(low, step) + pad_top(raw[HD:].astype(F32))


def invert(lowers):
    row = lax.broadcasted_iota(jnp.int32, (CHUNK, CHUNK), 0)
    col = lax.broadcasted_iota(jnp.int32, (CHUNK, CHUNK), 1)

    def pick(low, bits):
        r, c = lax.shift_right_logical(row, bits), lax.shift_right_logical(col, bits)
        mask = (lax.bitwise_and(r, 1) == 1) & (c == r - 1)
        return jnp.where(mask, low, 0.0)

    eye = (row == col).astype(F32)
    inverses = [eye - pick(low, 0) for low in lowers]
    bits = 1
    while (1 << bits) < CHUNK:
        first = [mm3(x, pick(low, bits)) for x, low in zip(inverses, lowers)]
        inverses = [x - mm3(f, x) for x, f in zip(inverses, first)]
        bits += 1
    return inverses


def layer(
    x_chips, z_chips,
    tok, wq, wk, wv, wb_in, bias_in, conv_in, gain_in, wo,
    out,
    wb, bias, conv, gain,
    gathered, halo, weights, outw, padded, logits,
    q_eff, o_loc, ring, lines, left, right, own_f, prefix, duo, mate, next_state, state, entering,
    give, got,
    load_sem, tok_send, tok_recv, halo_send, halo_recv, w_send, w_recv,
    duo_send, duo_recv, ring_send, ring_recv, line_send, line_recv, give_send, got_recv,
):
    s, h = lax.axis_index("seq"), lax.axis_index("head")
    shards = x_chips * z_chips
    y, c = h // 2, h % 2
    x, z = s // z_chips, s % z_chips
    up, down, far = (y + 1) % Y_CHIPS, (y + 3) % Y_CHIPS, (y + 2) % Y_CHIPS
    other = 1 - c

    def head_of(yy, cc):
        return yy * 2 + cc

    partner = (s, head_of(y, other))

    def remote(src, dst, send, recv, device):
        return pltpu.make_async_remote_copy(
            src_ref=src, dst_ref=dst, send_sem=send, recv_sem=recv,
            device_id=device, device_id_type=MESH,
        )

    def arrived(dst, recv):
        remote(dst, dst, recv, recv, partner).wait_recv()

    def settle(shape_of, sem):
        pltpu.make_async_copy(shape_of, shape_of, sem).wait()

    loads = [
        pltpu.make_async_copy(w, weights.at[:, pl.ds(i * HD, HD)], load_sem.at[0])
        for i, w in enumerate((wq, wk, wv))
    ]
    own_wo = pltpu.make_async_copy(wo, outw.at[h], load_sem.at[1])
    small = [
        pltpu.make_async_copy(src, dst, load_sem.at[3 + i])
        for i, (src, dst) in enumerate(
            ((wb_in, wb), (bias_in, bias), (conv_in, conv), (gain_in, gain))
        )
    ]
    own_tok = [
        pltpu.make_async_copy(
            tok.at[pl.ds(i * PART, PART)], gathered.at[y, c, i], load_sem.at[2]
        )
        for i in range(4)
    ]
    for copy in (*own_tok, *small, *loads, own_wo):
        copy.start()

    barrier = pltpu.get_barrier_semaphore()

    def greet(device):
        pl.semaphore_signal(barrier, inc=1, device_id=device, device_id_type=MESH)

    for step in range(1, 8):
        greet((s, (h + step) % 8))
    near = [z + 1 - 2 * (z % 2)]
    for offset in (2, 4) if z_chips == 16 else (2,):
        near += [(z + offset) % z_chips, (z + z_chips - offset) % z_chips]
    for hops in near:
        greet((x * z_chips + hops, h))
    for step in range(1, x_chips):
        greet((((x + step) % x_chips) * z_chips + z, h))

    @pl.when(s > 0)
    def _():
        greet((s - 1, 7))

    sends_halo = (h == 7) & (s < shards - 1)

    @pl.when(sends_halo)
    def _():
        for peer in range(8):
            greet((s + 1, peer))

    pl.semaphore_wait(
        barrier,
        7 + len(near) + (x_chips - 1) + jnp.where(s > 0, 1, 0) + jnp.where(sends_halo, 8, 0),
    )

    def tok_copy(src, yy, cc, part, device, kind):
        recv = tok_recv.at[yy, 4] if device is partner else tok_recv.at[yy, part]
        remote(src, gathered.at[yy, cc, part], tok_send.at[kind], recv, device).start()

    def relay(yy, half, device):
        tok_copy(gathered.at[yy, c, half], yy, c, half, device, 1)

    to_up, to_down = (s, head_of(up, c)), (s, head_of(down, c))
    settle(gathered.at[y, c], load_sem.at[2])
    own = [gathered.at[y, c, i] for i in range(4)]
    for first, second in ((0, 2), (1, 3), (2, 0), (3, 1)):
        tok_copy(own[first], y, c, first, to_up, 0)
        tok_copy(own[second], y, c, second, to_down, 0)
    for i in range(4):
        tok_copy(own[i], y, c, i, partner, 0)

    def halo_copy(peer):
        return remote(
            tok.at[pl.ds(ROWS - HALO, HALO)], halo, halo_send, halo_recv, (s + 1, peer)
        )

    @pl.when(sends_halo)
    def _():
        for peer in range(8):
            halo_copy(peer).start()

    @pl.when(s == 0)
    def _():
        halo[...] = jnp.zeros_like(halo)

    for copy in small:
        copy.wait()
    rate_rows = jnp.broadcast_to(wb[...].astype(F32), (HD, D))
    weights[:, pl.ds(3 * HD, HD)] = jnp.transpose(rate_rows).astype(BF16)
    settle(weights.at[:, pl.ds(0, 3 * HD)], load_sem.at[0])

    def project(yy):
        block = gathered[yy].reshape(CHUNK, D)
        result = dot(block, weights[...])
        start = pl.multiple_of(yy * CHUNK, CHUNK)
        padded[pl.ds(start + HALO, CHUNK), :] = result[:, : 3 * HD].astype(BF16).astype(F32)
        logits[pl.ds(start, CHUNK), :] = result[:, 3 * HD :]

    def tok_arrived(yy, part):
        arrived(gathered.at[yy, c, part], tok_recv.at[yy, part])

    def tok_other_arrived(yy):
        arrived(gathered.at[yy, other], tok_recv.at[yy, 4])

    def near_arrived(up_part, down_part, onward):
        tok_arrived(down, up_part)
        if onward:
            relay(down, up_part, to_up)
        relay(down, up_part, partner)
        tok_arrived(up, down_part)
        if onward:
            relay(up, down_part, to_down)
        relay(up, down_part, partner)

    near_arrived(0, 2, True)
    near_arrived(1, 3, True)
    tok_other_arrived(y)
    project(y)
    near_arrived(2, 0, False)
    near_arrived(3, 1, False)
    @pl.when(s > 0)
    def _():
        arrived(halo, halo_recv)

    edge = dot(halo[...], weights[...])[:, : 3 * HD].astype(BF16).astype(F32)
    padded[pl.ds(0, HALO), :] = edge
    for part in (0, 2, 1, 3):
        tok_arrived(far, part)
        relay(far, part, partner)
    for yy in (down, up):
        tok_other_arrived(yy)
        project(yy)
    tok_other_arrived(far)
    project(far)

    own_wo.wait()

    def wo_copy(src, slot, half, device):
        rows = pl.ds(half * ROWS, ROWS)
        recv = w_recv.at[slot // 2, 2 if device is partner else half]
        remote(src.at[rows], outw.at[slot, rows], w_send, recv, device).start()

    def wo_relay(yy, half, device):
        slot = head_of(yy, c)
        wo_copy(outw.at[slot], slot, half, device)

    def wo_arrived(yy, half):
        slot = head_of(yy, c)
        arrived(outw.at[slot, pl.ds(half * ROWS, ROWS)], w_recv.at[yy, half])

    wo_copy(outw.at[h], h, 0, to_up)
    wo_copy(outw.at[h], h, 1, to_down)
    wo_copy(outw.at[h], h, 1, to_up)
    wo_copy(outw.at[h], h, 0, to_down)
    wo_copy(outw.at[h], h, 0, partner)
    wo_copy(outw.at[h], h, 1, partner)

    def wo_relay_near():
        for yy, first, onward in ((down, 0, to_up), (up, 1, to_down)):
            wo_arrived(yy, first)
            wo_relay(yy, first, onward)
        for yy in (down, up):
            for half in range(2):
                if (yy is down) == (half == 1):
                    wo_arrived(yy, half)
                wo_relay(yy, half, partner)

    def wo_relay_far():
        for half in range(2):
            wo_arrived(far, half)
            wo_relay(far, half, partner)

    row = lax.broadcasted_iota(jnp.int32, (CHUNK, CHUNK), 0)
    col = lax.broadcasted_iota(jnp.int32, (CHUNK, CHUNK), 1)
    parts, lowers, rights, attends = [], [], [], []
    for n in range(CHUNKS):
        base = n * CHUNK
        acts = []
        for i in range(3):
            lanes = pl.ds(i * HD, HD)
            total = padded[pl.ds(base + HALO - 3, CHUNK), lanes] * conv[i, 0:1]
            for j in range(1, 4):
                total = total + padded[pl.ds(base + HALO - 3 + j, CHUNK), lanes] * conv[i, j : j + 1]
            acts.append((total / (1.0 + jnp.exp(-total))).astype(BF16))
        query, key, value = acts
        key32 = key.astype(F32)
        inv = 1.0 / jnp.sqrt(jnp.sum(key32 * key32, -1, keepdims=True) + 1e-06)
        beta = 2.0 * jax.nn.sigmoid(logits[pl.ds(base, CHUNK), :] + bias[0])
        rate = beta * inv
        gram = dot(key, key, NT)
        lowers.append(jnp.where(row > col, (rate * inv) * gram, 0.0))
        rights.append(
            jnp.concatenate([(rate * inv) * key32, rate * value.astype(F32)], 1)
        )
        attends.append(jnp.where(row >= col, dot(query, key, NT), 0.0).astype(BF16))
        parts.append((query, key))
    inverses = invert(lowers)
    eye = (row == col).astype(F32)
    lead = jnp.concatenate([eye, jnp.zeros((HD, HD), F32)], 0)
    before, entry, reached = lead, [], []
    for n in range(CHUNKS):
        query, key = parts[n]
        solved = mm3(inverses[n], rights[n])
        high, low = split(solved)
        moved = dot(high, key, TN) + dot(low, key, TN)
        step = jnp.concatenate([eye - moved[:HD], moved[HD:]], 0)
        entry.append(before)
        reached.append(high)
        before = step if n == 0 else after(before, step)

    def finish_outputs():
        for n in range(CHUNKS):
            reach = dot(attends[n], reached[n])
            eff = (parts[n][0].astype(F32) - reach[:, :HD]).astype(BF16)
            if n == 0:
                q_eff[pl.ds(0, CHUNK), :] = eff
                o_loc[pl.ds(0, CHUNK), :] = reach[:, HD:]
            else:
                turned = dot(eff, entry[n].astype(BF16), NT)
                q_eff[pl.ds(n * CHUNK, CHUNK), :] = turned[:, :HD].astype(BF16)
                o_loc[pl.ds(n * CHUNK, CHUNK), :] = turned[:, HD:] + reach[:, HD:]


    odd = z % 2
    pairs = z_chips // 2
    j = z // 2

    def at_z(offset):
        return (x * z_chips + (z + z_chips + offset) % z_chips, h)

    duo[...] = before.astype(BF16)
    to_even = remote(duo, mate, duo_send.at[0], duo_recv.at[0], at_z(-1))
    to_odd = remote(next_state, next_state, duo_send.at[1], duo_recv.at[1], at_z(1))

    @pl.when(odd == 1)
    def _():
        to_even.start()

    finish_outputs()

    def ring_copy(slot, q, offset, sem):
        remote(
            ring.at[slot, q], ring.at[slot, q], ring_send, ring_recv.at[slot, sem],
            at_z(2 * offset),
        ).start()

    def compose(k):
        slot = (j + pairs - k) % pairs
        side = jnp.where(k > j, 1, 0)
        left[side] = prepend(ring[slot].reshape(2 * HD, HD), left[side])
        if 2 * k < pairs:
            slot_r = (j + k) % pairs
            side_r = jnp.where(j + k >= pairs, 1, 0)
            right[side_r] = append(right[side_r], ring[slot_r].reshape(2 * HD, HD))

    def ring_arrived(k):
        if 2 * k < pairs:
            for slot in ((j + pairs - k) % pairs, (j + k) % pairs):
                arrived(ring.at[slot], ring_recv.at[slot, 0])
        else:
            slot = (j + k) % pairs
            for side in range(2):
                arrived(ring.at[slot, pl.ds(side * HALF_SUBS, HALF_SUBS)], ring_recv.at[slot, side])

    def scan_pairs():
        for i in range(2):
            left[i] = lead
            right[i] = lead
        arrived(mate, duo_recv.at[0])
        own_f[...] = append(before, mate[...])
        ring[j] = own_f[...].astype(BF16).reshape(SUBS, 2 * HD // SUBS, HD)
        if pairs == 8:
            for q in range(SUBS):
                ring_copy(j, q, 2, q)
                ring_copy(j, q, -2, q)
            for q in range(SUBS):
                ring_copy(j, q, 1, 0)
                ring_copy(j, q, -1, 0)
            back, ahead = (j + pairs - 2) % pairs, (j + 2) % pairs
            for q in range(SUBS):
                arrived(ring.at[back, q], ring_recv.at[back, q])
                if q < HALF_SUBS:
                    ring_copy(back, q, 2, 0)
                ring_copy(back, q, 1, 0)
                arrived(ring.at[ahead, q], ring_recv.at[ahead, q])
                if q >= HALF_SUBS:
                    ring_copy(ahead, q, -2, 1)
                ring_copy(ahead, q, -1, 0)
            wo_relay_near()
            ring_arrived(1)
            compose(1)
            compose(2)
            wo_relay_far()
            ring_arrived(3)
            compose(3)
        else:
            for q in range(SUBS):
                ring_copy(j, q, 1 if q < HALF_SUBS else -1, q // HALF_SUBS)
            wo_relay_near()
            wo_relay_far()
        ring_arrived(pairs // 2)
        compose(pairs // 2)
        prefix[...] = after(right[1], left[0])
        line = after(prefix[...], after(own_f[...], after(right[0], left[1])))

        lines[x] = line.astype(BF16).reshape(2, HD, HD)
        moves = [
            (0, 2, 1), (0, 1, 1), (0, 3, 1), (1, 3, 0), (1, 3, 1),
            (1, 2, 0), (1, 2, 1), (2, 3, 0), (2, 3, 1),
        ]

        def line_copy(i):
            slot, to, part = moves[i]
            return remote(
                lines.at[slot, part], lines.at[slot, part], line_send,
                line_recv.at[slot, part], (to * z_chips + z, h),
            )

        def line_arrived(slot, part):
            arrived(lines.at[slot, part], line_recv.at[slot, part])

        if x_chips == 4:
            for i, move in enumerate(moves):

                @pl.when(x == move[0])
                def _():
                    line_copy(i).start()

        entering[...] = jnp.zeros_like(entering)
        for k in range(x_chips - 1):

            @pl.when(k < x)
            def _():
                line_arrived(k, 1)
                if k == 0:
                    entering[...] = lines[0, 1].astype(F32)
                else:
                    line_arrived(k, 0)
                    high, low = split(entering[...])
                    step = lines[k, 0]
                    entering[...] = dot(high, step) + dot(low, step) + lines[k, 1].astype(F32)

        own_in = mm3(entering[...], prefix[pl.ds(0, HD)]) + prefix[pl.ds(HD, HD)]
        next_state[...] = (mm3(own_in, before[:HD]) + before[HD:]).astype(BF16)
        to_odd.start()
        state[...] = own_in

    @pl.when(odd == 0)
    def _():
        scan_pairs()

    @pl.when(odd == 1)
    def _():
        wo_relay_near()
        wo_relay_far()
        arrived(next_state, duo_recv.at[1])
        state[...] = next_state[...].astype(F32)

    high, low = split(state[...])
    outputs = dot(q_eff[...], high, NT) + dot(q_eff[...], low, NT) + o_loc[...]
    scale = lax.rsqrt(jnp.mean(outputs * outputs, -1, keepdims=True) + 1e-05)
    normed = (outputs * scale * gain[...]).astype(BF16)
    for peer in range(8):
        give[peer] = normed[peer * ROWS : (peer + 1) * ROWS]
    order = [head_of(yy, cc) for yy, cc in (
        (far, c), (far, other), (up, c), (down, c), (up, other), (down, other), (y, other)
    )]
    for peer in order:
        remote(give.at[peer], got.at[h], give_send, got_recv, (s, peer)).start()
    got[h] = give[h]
    for yy in (y, up, down, far):
        arrived(outw.at[head_of(yy, other)], w_recv.at[yy, 2])
    settle(got.at[pl.ds(0, 7)], got_recv)
    mixed = jnp.zeros((ROWS, D), F32)
    for g in range(8):
        mixed = mixed + dot(got[g], outw[g]).astype(BF16).astype(F32)
    out[...] = mixed.astype(BF16)

    settle(gathered.at[pl.ds(0, 3), 0], tok_send.at[0])
    settle(gathered.at[:, 0], tok_send.at[1])
    settle(outw.at[pl.ds(0, 7)], w_send)
    settle(give.at[pl.ds(0, 7)], give_send)

    @pl.when(odd == 1)
    def _():
        to_even.wait_send()

    @pl.when(odd == 0)
    def _():
        to_odd.wait_send()
        settle(ring.at[pl.ds(0, RING_SENDS[pairs])], ring_send)

    if x_chips == 4:
        for line_x, count in enumerate((3, 4, 2)):

            @pl.when((odd == 0) & (x == line_x))
            def _():
                settle(lines.at[pl.ds(0, count), 0], line_send)

    @pl.when(sends_halo)
    def _():
        settle(gathered.at[0, 0], halo_send)


def local(x_chips, z_chips, tokens, w_query, w_key, w_value, w_beta, beta_bias, conv_weight, norm_gain, w_out):
    hbm = pl.BlockSpec(memory_space=pltpu.HBM)
    vmem = pl.BlockSpec(memory_space=pltpu.VMEM)
    dma = pltpu.SemaphoreType.DMA
    return pl.pallas_call(
        functools.partial(layer, x_chips, z_chips),
        out_shape=jax.ShapeDtypeStruct((ROWS, D), BF16),
        in_specs=[hbm] * 9,
        out_specs=vmem,
        scratch_shapes=[
            pltpu.VMEM((1, D), BF16),
            pltpu.SMEM((1,), F32),
            pltpu.VMEM((3, 4, HD), F32),
            pltpu.VMEM((1, HD), F32),
            pltpu.VMEM((Y_CHIPS, 2, 4, PART, D), BF16),
            pltpu.VMEM((HALO, D), BF16),
            pltpu.VMEM((D, 4 * HD), BF16),
            pltpu.VMEM((8, HD, D), BF16),
            pltpu.VMEM((HALO + SHARD, 3 * HD), F32),
            pltpu.VMEM((SHARD, HD), F32),
            pltpu.VMEM((SHARD, HD), BF16),
            pltpu.VMEM((SHARD, HD), F32),
            pltpu.VMEM((z_chips // 2, SUBS, 2 * HD // SUBS, HD), BF16),
            pltpu.VMEM((x_chips, 2, HD, HD), BF16),
            pltpu.VMEM((2, 2 * HD, HD), F32),
            pltpu.VMEM((2, 2 * HD, HD), F32),
            pltpu.VMEM((2 * HD, HD), F32),
            pltpu.VMEM((2 * HD, HD), F32),
            pltpu.VMEM((2 * HD, HD), BF16),
            pltpu.VMEM((2 * HD, HD), BF16),
            pltpu.VMEM((HD, HD), BF16),
            pltpu.VMEM((HD, HD), F32),
            pltpu.VMEM((HD, HD), F32),
            pltpu.VMEM((8, ROWS, HD), BF16),
            pltpu.VMEM((8, ROWS, HD), BF16),
            dma((7,)),
            dma((2,)),
            dma((Y_CHIPS, 5)),
            dma,
            dma,
            dma,
            dma((Y_CHIPS, 3)),
            dma((2,)),
            dma((2,)),
            dma,
            dma((z_chips // 2, SUBS)),
            dma,
            dma((x_chips, 2)),
            dma,
            dma,
        ],
        compiler_params=pltpu.CompilerParams(
            collective_id=0, has_side_effects=True, vmem_limit_bytes=48 * 1024 * 1024
        ),
    )(
        keep(tokens), keep(w_query), keep(w_key), keep(w_value),
        keep(w_beta.reshape(1, D)), beta_bias, keep(conv_weight),
        keep(norm_gain.reshape(1, HD)), keep(w_out),
    )


def keep(a):
    return pltpu.with_memory_space_constraint(a, pltpu.HBM)


def solution(mesh):
    z_chips = Z_CHIPS
    x_chips = mesh.shape["seq"] // z_chips
    in_specs = (
        P(("seq", "head"), None),
        P(None, "head"),
        P(None, "head"),
        P(None, "head"),
        P(None, "head"),
        P("head"),
        P(None, None, "head"),
        P("head"),
        P("head", None),
    )
    out_specs = P(("seq", "head"), None)
    return jax.shard_map(
        functools.partial(local, x_chips, z_chips),
        mesh=mesh, in_specs=in_specs, out_specs=out_specs, check_vma=False,
    )
```

```python
import functools

import jax
import jax.numpy as jnp
from jax import lax
from jax.experimental import pallas as pl
from jax.experimental.pallas import tpu as pltpu
from jax.sharding import PartitionSpec as P

F32, BF16 = jnp.float32, jnp.bfloat16
MESH = pl.DeviceIdType.MESH
Z_CHIPS = 16
Y_CHIPS = 4
D = 1024
HD = 128
ROWS = 64
SHARD = 512
CHUNK = 128
CHUNKS = SHARD // CHUNK
PART = 16
HALO = 8
SUBS = 4
HALF_SUBS = SUBS // 2
RING_SENDS = {2: 1, 8: 7}

NN = (((1,), (0,)), ((), ()))
NT = (((1,), (1,)), ((), ()))
TN = (((0,), (0,)), ((), ()))


def dot(a, b, dims=NN):
    return lax.dot_general(a, b, dims, preferred_element_type=F32)


def split(a):
    high = a.astype(BF16)
    return high, (a - high.astype(F32)).astype(BF16)


def mm3(a, b):
    bh, bl = split(b)
    wide = b.shape[1]
    pair = jnp.concatenate([bh, bl], 1)
    alone = jnp.concatenate([bh, jnp.zeros_like(bh)], 1)
    both = dot(jnp.concatenate(split(a), 1), jnp.concatenate([pair, alone], 0))
    return both[:, :wide] + both[:, wide:]


def after(earlier, later):
    return mm3(earlier, later[:HD]) + pad_top(later[HD:])


def pad_top(state):
    return jnp.concatenate([jnp.zeros((HD, HD), F32), state], 0)


def prepend(raw, acc):
    both = dot(raw, jnp.concatenate(split(acc[:HD]), 1))
    return both[:, :HD] + both[:, HD:] + pad_top(acc[HD:])


def twice(a, b):
    return dot(jnp.concatenate(split(a), 1), jnp.concatenate([b, b], 0))


def append(acc, raw):
    return twice(acc, raw[:HD]) + pad_top(raw[HD:].astype(F32))


def invert(lowers):
    row = lax.broadcasted_iota(jnp.int32, (CHUNK, CHUNK), 0)
    col = lax.broadcasted_iota(jnp.int32, (CHUNK, CHUNK), 1)

    def pick(low, bits):
        r, c = lax.shift_right_logical(row, bits), lax.shift_right_logical(col, bits)
        mask = (lax.bitwise_and(r, 1) == 1) & (c == r - 1)
        return jnp.where(mask, low, 0.0)

    eye = (row == col).astype(F32)
    inverses = [eye - pick(low, 0) for low in lowers]
    bits = 1
    while (1 << bits) < CHUNK:
        first = [mm3(x, pick(low, bits)) for x, low in zip(inverses, lowers)]
        inverses = [x - mm3(f, x) for x, f in zip(inverses, first)]
        bits += 1
    return inverses


def layer(
    x_chips, z_chips,
    tok, wq, wk, wv, wb_in, bias_in, conv_in, gain_in, wo,
    out,
    wb, bias, conv, gain,
    gathered, halo, weights, outw, padded, logits,
    q_eff, o_loc, ring, lines, left, right, own_f, prefix, duo, mate, next_state, state, entering,
    give, got,
    load_sem, tok_send, tok_recv, halo_send, halo_recv, w_send, w_recv,
    duo_send, duo_recv, ring_send, ring_recv, line_send, line_recv, give_send, got_recv,
):
    s, h = lax.axis_index("seq"), lax.axis_index("head")
    shards = x_chips * z_chips
    y, c = h // 2, h % 2
    x, z = s // z_chips, s % z_chips
    up, down, far = (y + 1) % Y_CHIPS, (y + 3) % Y_CHIPS, (y + 2) % Y_CHIPS
    other = 1 - c

    def head_of(yy, cc):
        return yy * 2 + cc

    partner = (s, head_of(y, other))

    def remote(src, dst, send, recv, device):
        return pltpu.make_async_remote_copy(
            src_ref=src, dst_ref=dst, send_sem=send, recv_sem=recv,
            device_id=device, device_id_type=MESH,
        )

    def arrived(dst, recv):
        remote(dst, dst, recv, recv, partner).wait_recv()

    def settle(shape_of, sem):
        pltpu.make_async_copy(shape_of, shape_of, sem).wait()

    loads = [
        pltpu.make_async_copy(w, weights.at[:, pl.ds(i * HD, HD)], load_sem.at[0])
        for i, w in enumerate((wq, wk, wv))
    ]
    own_wo = pltpu.make_async_copy(wo, outw.at[h], load_sem.at[1])
    small = [
        pltpu.make_async_copy(src, dst, load_sem.at[3 + i])
        for i, (src, dst) in enumerate(
            ((wb_in, wb), (bias_in, bias), (conv_in, conv), (gain_in, gain))
        )
    ]
    own_tok = [
        pltpu.make_async_copy(
            tok.at[pl.ds(i * PART, PART)], gathered.at[y, c, i], load_sem.at[2]
        )
        for i in range(4)
    ]
    for copy in (*own_tok, *small, *loads, own_wo):
        copy.start()

    barrier = pltpu.get_barrier_semaphore()

    def greet(device):
        pl.semaphore_signal(barrier, inc=1, device_id=device, device_id_type=MESH)

    for step in range(1, 8):
        greet((s, (h + step) % 8))
    near = [z + 1 - 2 * (z % 2)]
    for offset in (2, 4) if z_chips == 16 else (2,):
        near += [(z + offset) % z_chips, (z + z_chips - offset) % z_chips]
    for hops in near:
        greet((x * z_chips + hops, h))
    for step in range(1, x_chips):
        greet((((x + step) % x_chips) * z_chips + z, h))

    @pl.when(s > 0)
    def _():
        greet((s - 1, 7))

    sends_halo = (h == 7) & (s < shards - 1)

    @pl.when(sends_halo)
    def _():
        for peer in range(8):
            greet((s + 1, peer))

    pl.semaphore_wait(
        barrier,
        7 + len(near) + (x_chips - 1) + jnp.where(s > 0, 1, 0) + jnp.where(sends_halo, 8, 0),
    )

    def tok_copy(src, yy, cc, part, device, kind):
        recv = tok_recv.at[yy, 4] if device is partner else tok_recv.at[yy, part]
        remote(src, gathered.at[yy, cc, part], tok_send.at[kind], recv, device).start()

    def relay(yy, half, device):
        tok_copy(gathered.at[yy, c, half], yy, c, half, device, 1)

    to_up, to_down = (s, head_of(up, c)), (s, head_of(down, c))
    settle(gathered.at[y, c], load_sem.at[2])
    own = [gathered.at[y, c, i] for i in range(4)]
    for first, second in ((0, 2), (1, 3), (2, 0), (3, 1)):
        tok_copy(own[first], y, c, first, to_up, 0)
        tok_copy(own[second], y, c, second, to_down, 0)
    for i in range(4):
        tok_copy(own[i], y, c, i, partner, 0)

    def halo_copy(peer):
        return remote(
            tok.at[pl.ds(ROWS - HALO, HALO)], halo, halo_send, halo_recv, (s + 1, peer)
        )

    @pl.when(sends_halo)
    def _():
        for peer in range(8):
            halo_copy(peer).start()

    @pl.when(s == 0)
    def _():
        halo[...] = jnp.zeros_like(halo)

    for copy in small:
        copy.wait()
    rate_rows = jnp.broadcast_to(wb[...].astype(F32), (HD, D))
    weights[:, pl.ds(3 * HD, HD)] = jnp.transpose(rate_rows).astype(BF16)
    settle(weights.at[:, pl.ds(0, 3 * HD)], load_sem.at[0])

    def project(yy):
        block = gathered[yy].reshape(CHUNK, D)
        result = dot(block, weights[...])
        start = pl.multiple_of(yy * CHUNK, CHUNK)
        padded[pl.ds(start + HALO, CHUNK), :] = result[:, : 3 * HD].astype(BF16).astype(F32)
        logits[pl.ds(start, CHUNK), :] = result[:, 3 * HD :]

    def tok_arrived(yy, part):
        arrived(gathered.at[yy, c, part], tok_recv.at[yy, part])

    def tok_other_arrived(yy):
        arrived(gathered.at[yy, other], tok_recv.at[yy, 4])

    def near_arrived(up_part, down_part, onward):
        tok_arrived(down, up_part)
        if onward:
            relay(down, up_part, to_up)
        relay(down, up_part, partner)
        tok_arrived(up, down_part)
        if onward:
            relay(up, down_part, to_down)
        relay(up, down_part, partner)

    near_arrived(0, 2, True)
    near_arrived(1, 3, True)
    tok_other_arrived(y)
    project(y)
    near_arrived(2, 0, False)
    near_arrived(3, 1, False)
    @pl.when(s > 0)
    def _():
        arrived(halo, halo_recv)

    edge = dot(halo[...], weights[...])[:, : 3 * HD].astype(BF16).astype(F32)
    padded[pl.ds(0, HALO), :] = edge
    for part in (0, 2, 1, 3):
        tok_arrived(far, part)
        relay(far, part, partner)
    for yy in (down, up):
        tok_other_arrived(yy)
        project(yy)
    tok_other_arrived(far)
    project(far)

    own_wo.wait()

    def wo_copy(src, slot, half, device):
        rows = pl.ds(half * ROWS, ROWS)
        recv = w_recv.at[slot // 2, 2 if device is partner else half]
        remote(src.at[rows], outw.at[slot, rows], w_send, recv, device).start()

    def wo_relay(yy, half, device):
        slot = head_of(yy, c)
        wo_copy(outw.at[slot], slot, half, device)

    def wo_arrived(yy, half):
        slot = head_of(yy, c)
        arrived(outw.at[slot, pl.ds(half * ROWS, ROWS)], w_recv.at[yy, half])

    wo_copy(outw.at[h], h, 0, to_up)
    wo_copy(outw.at[h], h, 1, to_down)
    wo_copy(outw.at[h], h, 1, to_up)
    wo_copy(outw.at[h], h, 0, to_down)
    wo_copy(outw.at[h], h, 0, partner)
    wo_copy(outw.at[h], h, 1, partner)

    def wo_relay_near():
        for yy, first, onward in ((down, 0, to_up), (up, 1, to_down)):
            wo_arrived(yy, first)
            wo_relay(yy, first, onward)
        for yy in (down, up):
            for half in range(2):
                if (yy is down) == (half == 1):
                    wo_arrived(yy, half)
                wo_relay(yy, half, partner)

    def wo_relay_far():
        for half in range(2):
            wo_arrived(far, half)
            wo_relay(far, half, partner)

    row = lax.broadcasted_iota(jnp.int32, (CHUNK, CHUNK), 0)
    col = lax.broadcasted_iota(jnp.int32, (CHUNK, CHUNK), 1)
    parts, lowers, rights, attends = [], [], [], []
    for n in range(CHUNKS):
        base = n * CHUNK
        acts = []
        for i in range(3):
            lanes = pl.ds(i * HD, HD)
            total = padded[pl.ds(base + HALO - 3, CHUNK), lanes] * conv[i, 0:1]
            for j in range(1, 4):
                total = total + padded[pl.ds(base + HALO - 3 + j, CHUNK), lanes] * conv[i, j : j + 1]
            acts.append((total / (1.0 + jnp.exp(-total))).astype(BF16))
        query, key, value = acts
        key32 = key.astype(F32)
        inv = 1.0 / jnp.sqrt(jnp.sum(key32 * key32, -1, keepdims=True) + 1e-06)
        beta = 2.0 * jax.nn.sigmoid(logits[pl.ds(base, CHUNK), :] + bias[0])
        rate = beta * inv
        gram = dot(key, key, NT)
        lowers.append(jnp.where(row > col, (rate * inv) * gram, 0.0))
        rights.append(
            jnp.concatenate([(rate * inv) * key32, rate * value.astype(F32)], 1)
        )
        attends.append(jnp.where(row >= col, dot(query, key, NT), 0.0).astype(BF16))
        parts.append((query, key))
    inverses = invert(lowers)
    eye = (row == col).astype(F32)
    lead = jnp.concatenate([eye, jnp.zeros((HD, HD), F32)], 0)
    before, entry, reached = lead, [], []
    for n in range(CHUNKS):
        query, key = parts[n]
        solved = mm3(inverses[n], rights[n])
        high, low = split(solved)
        moved = dot(jnp.concatenate([high, low], 0), jnp.concatenate([key, key], 0), TN)
        step = jnp.concatenate([eye - moved[:HD], moved[HD:]], 0)
        entry.append(before)
        reached.append(high)
        before = step if n == 0 else after(before, step)

    def finish_outputs():
        for n in range(CHUNKS):
            reach = dot(attends[n], reached[n])
            eff = (parts[n][0].astype(F32) - reach[:, :HD]).astype(BF16)
            if n == 0:
                q_eff[pl.ds(0, CHUNK), :] = eff
                o_loc[pl.ds(0, CHUNK), :] = reach[:, HD:]
            else:
                turned = dot(eff, entry[n].astype(BF16), NT)
                q_eff[pl.ds(n * CHUNK, CHUNK), :] = turned[:, :HD].astype(BF16)
                o_loc[pl.ds(n * CHUNK, CHUNK), :] = turned[:, HD:] + reach[:, HD:]


    odd = z % 2
    pairs = z_chips // 2
    j = z // 2

    def at_z(offset):
        return (x * z_chips + (z + z_chips + offset) % z_chips, h)

    duo[...] = before.astype(BF16)
    to_even = remote(duo, mate, duo_send.at[0], duo_recv.at[0], at_z(-1))
    to_odd = remote(next_state, next_state, duo_send.at[1], duo_recv.at[1], at_z(1))

    @pl.when(odd == 1)
    def _():
        to_even.start()

    finish_outputs()

    def ring_copy(slot, q, offset, sem):
        remote(
            ring.at[slot, q], ring.at[slot, q], ring_send, ring_recv.at[slot, sem],
            at_z(2 * offset),
        ).start()

    def compose(k):
        slot = (j + pairs - k) % pairs
        side = jnp.where(k > j, 1, 0)
        left[side] = prepend(ring[slot].reshape(2 * HD, HD), left[side])
        if 2 * k < pairs:
            slot_r = (j + k) % pairs
            side_r = jnp.where(j + k >= pairs, 1, 0)
            right[side_r] = append(right[side_r], ring[slot_r].reshape(2 * HD, HD))

    def ring_arrived(k):
        if 2 * k < pairs:
            for slot in ((j + pairs - k) % pairs, (j + k) % pairs):
                arrived(ring.at[slot], ring_recv.at[slot, 0])
        else:
            slot = (j + k) % pairs
            for side in range(2):
                arrived(ring.at[slot, pl.ds(side * HALF_SUBS, HALF_SUBS)], ring_recv.at[slot, side])

    def scan_pairs():
        for i in range(2):
            left[i] = lead
            right[i] = lead
        arrived(mate, duo_recv.at[0])
        own_f[...] = append(before, mate[...])
        ring[j] = own_f[...].astype(BF16).reshape(SUBS, 2 * HD // SUBS, HD)
        if pairs == 8:
            for q in range(SUBS):
                ring_copy(j, q, 2, q)
                ring_copy(j, q, -2, q)
            for q in range(SUBS):
                ring_copy(j, q, 1, 0)
                ring_copy(j, q, -1, 0)
            back, ahead = (j + pairs - 2) % pairs, (j + 2) % pairs
            for q in range(SUBS):
                arrived(ring.at[back, q], ring_recv.at[back, q])
                if q < HALF_SUBS:
                    ring_copy(back, q, 2, 0)
                ring_copy(back, q, 1, 0)
                arrived(ring.at[ahead, q], ring_recv.at[ahead, q])
                if q >= HALF_SUBS:
                    ring_copy(ahead, q, -2, 1)
                ring_copy(ahead, q, -1, 0)
            wo_relay_near()
            ring_arrived(1)
            compose(1)
            compose(2)
            wo_relay_far()
            ring_arrived(3)
            compose(3)
        else:
            for q in range(SUBS):
                ring_copy(j, q, 1 if q < HALF_SUBS else -1, q // HALF_SUBS)
            wo_relay_near()
            wo_relay_far()
        ring_arrived(pairs // 2)
        compose(pairs // 2)
        prefix[...] = after(right[1], left[0])
        line = after(prefix[...], after(own_f[...], after(right[0], left[1])))

        lines[x] = line.astype(BF16).reshape(2, HD, HD)
        moves = [
            (0, 2, 1), (0, 1, 1), (0, 3, 1), (1, 3, 0), (1, 3, 1),
            (1, 2, 0), (1, 2, 1), (2, 3, 0), (2, 3, 1),
        ]

        def line_copy(i):
            slot, to, part = moves[i]
            return remote(
                lines.at[slot, part], lines.at[slot, part], line_send,
                line_recv.at[slot, part], (to * z_chips + z, h),
            )

        def line_arrived(slot, part):
            arrived(lines.at[slot, part], line_recv.at[slot, part])

        if x_chips == 4:
            for i, move in enumerate(moves):

                @pl.when(x == move[0])
                def _():
                    line_copy(i).start()

        entering[...] = jnp.zeros_like(entering)
        for k in range(x_chips - 1):

            @pl.when(k < x)
            def _():
                line_arrived(k, 1)
                if k == 0:
                    entering[...] = lines[0, 1].astype(F32)
                else:
                    line_arrived(k, 0)
                    entering[...] = twice(entering[...], lines[k, 0]) + lines[k, 1].astype(F32)

        own_in = mm3(entering[...], prefix[pl.ds(0, HD)]) + prefix[pl.ds(HD, HD)]
        next_state[...] = (mm3(own_in, before[:HD]) + before[HD:]).astype(BF16)
        to_odd.start()
        state[...] = own_in

    @pl.when(odd == 0)
    def _():
        scan_pairs()

    @pl.when(odd == 1)
    def _():
        wo_relay_near()
        wo_relay_far()
        arrived(next_state, duo_recv.at[1])
        state[...] = next_state[...].astype(F32)

    terms = jnp.concatenate(split(state[...]), 0)
    for yy in (far, up, down, y):
        rows = pl.ds(pl.multiple_of(yy * CHUNK, CHUNK), CHUNK)
        both = dot(q_eff[rows, :], terms, NT)
        outputs = both[:, :HD] + both[:, HD:] + o_loc[rows, :]
        scale = lax.rsqrt(jnp.mean(outputs * outputs, -1, keepdims=True) + 1e-05)
        give[yy] = (outputs * scale * gain[...]).astype(BF16).reshape(2, ROWS, HD)
        for cc in (c, other) if yy is not y else (other,):
            remote(
                give.at[yy, cc], got.at[h], give_send, got_recv.at[h], (s, head_of(yy, cc))
            ).start()
    got[h] = give[y, c]
    for yy in (y, up, down, far):
        arrived(outw.at[head_of(yy, other)], w_recv.at[yy, 2])
    mixed = dot(got[h], outw[h]).astype(BF16).astype(F32)
    for peer in (
        head_of(y, other), head_of(up, c), head_of(down, c), head_of(up, other),
        head_of(down, other), head_of(far, c), head_of(far, other),
    ):
        arrived(got.at[peer], got_recv.at[peer])
        mixed = mixed + dot(got[peer], outw[peer]).astype(BF16).astype(F32)
    out[...] = mixed.astype(BF16)

    settle(gathered.at[pl.ds(0, 3), 0], tok_send.at[0])
    settle(gathered.at[:, 0], tok_send.at[1])
    settle(outw.at[pl.ds(0, 7)], w_send)
    settle(got.at[pl.ds(0, 7)], give_send)

    @pl.when(odd == 1)
    def _():
        to_even.wait_send()

    @pl.when(odd == 0)
    def _():
        to_odd.wait_send()
        settle(ring.at[pl.ds(0, RING_SENDS[pairs])], ring_send)

    if x_chips == 4:
        for line_x, count in enumerate((3, 4, 2)):

            @pl.when((odd == 0) & (x == line_x))
            def _():
                settle(lines.at[pl.ds(0, count), 0], line_send)

    @pl.when(sends_halo)
    def _():
        settle(gathered.at[0, 0], halo_send)


def local(x_chips, z_chips, tokens, w_query, w_key, w_value, w_beta, beta_bias, conv_weight, norm_gain, w_out):
    hbm = pl.BlockSpec(memory_space=pltpu.HBM)
    vmem = pl.BlockSpec(memory_space=pltpu.VMEM)
    dma = pltpu.SemaphoreType.DMA
    return pl.pallas_call(
        functools.partial(layer, x_chips, z_chips),
        out_shape=jax.ShapeDtypeStruct((ROWS, D), BF16),
        in_specs=[hbm] * 9,
        out_specs=vmem,
        scratch_shapes=[
            pltpu.VMEM((1, D), BF16),
            pltpu.SMEM((1,), F32),
            pltpu.VMEM((3, 4, HD), F32),
            pltpu.VMEM((1, HD), F32),
            pltpu.VMEM((Y_CHIPS, 2, 4, PART, D), BF16),
            pltpu.VMEM((HALO, D), BF16),
            pltpu.VMEM((D, 4 * HD), BF16),
            pltpu.VMEM((8, HD, D), BF16),
            pltpu.VMEM((HALO + SHARD, 3 * HD), F32),
            pltpu.VMEM((SHARD, HD), F32),
            pltpu.VMEM((SHARD, HD), BF16),
            pltpu.VMEM((SHARD, HD), F32),
            pltpu.VMEM((z_chips // 2, SUBS, 2 * HD // SUBS, HD), BF16),
            pltpu.VMEM((x_chips, 2, HD, HD), BF16),
            pltpu.VMEM((2, 2 * HD, HD), F32),
            pltpu.VMEM((2, 2 * HD, HD), F32),
            pltpu.VMEM((2 * HD, HD), F32),
            pltpu.VMEM((2 * HD, HD), F32),
            pltpu.VMEM((2 * HD, HD), BF16),
            pltpu.VMEM((2 * HD, HD), BF16),
            pltpu.VMEM((HD, HD), BF16),
            pltpu.VMEM((HD, HD), F32),
            pltpu.VMEM((HD, HD), F32),
            pltpu.VMEM((Y_CHIPS, 2, ROWS, HD), BF16),
            pltpu.VMEM((8, ROWS, HD), BF16),
            dma((7,)),
            dma((2,)),
            dma((Y_CHIPS, 5)),
            dma,
            dma,
            dma,
            dma((Y_CHIPS, 3)),
            dma((2,)),
            dma((2,)),
            dma,
            dma((z_chips // 2, SUBS)),
            dma,
            dma((x_chips, 2)),
            dma,
            dma((8,)),
        ],
        compiler_params=pltpu.CompilerParams(
            collective_id=0, has_side_effects=True, vmem_limit_bytes=48 * 1024 * 1024
        ),
    )(
        keep(tokens), keep(w_query), keep(w_key), keep(w_value),
        keep(w_beta.reshape(1, D)), beta_bias, keep(conv_weight),
        keep(norm_gain.reshape(1, HD)), keep(w_out),
    )


def keep(a):
    return pltpu.with_memory_space_constraint(a, pltpu.HBM)


def solution(mesh):
    z_chips = Z_CHIPS
    x_chips = mesh.shape["seq"] // z_chips
    in_specs = (
        P(("seq", "head"), None),
        P(None, "head"),
        P(None, "head"),
        P(None, "head"),
        P(None, "head"),
        P("head"),
        P(None, None, "head"),
        P("head"),
        P("head", None),
    )
    out_specs = P(("seq", "head"), None)
    return jax.shard_map(
        functools.partial(local, x_chips, z_chips),
        mesh=mesh, in_specs=in_specs, out_specs=out_specs, check_vma=False,
    )
```

```python
import functools

import jax
import jax.numpy as jnp
from jax import lax
from jax.experimental import pallas as pl
from jax.experimental.pallas import tpu as pltpu
from jax.sharding import PartitionSpec as P

F32, BF16 = jnp.float32, jnp.bfloat16
MESH = pl.DeviceIdType.MESH
Z_CHIPS = 16
Y_CHIPS = 4
D = 1024
HD = 128
ROWS = 64
SHARD = 512
CHUNK = 128
CHUNKS = SHARD // CHUNK
PART = 16
HALO = 8
SUBS = 4
HALF_SUBS = SUBS // 2
RING_SENDS = {2: 1, 8: 7}

NN = (((1,), (0,)), ((), ()))
NT = (((1,), (1,)), ((), ()))
TN = (((0,), (0,)), ((), ()))


def dot(a, b, dims=NN):
    return lax.dot_general(a, b, dims, preferred_element_type=F32)


def split(a):
    high = a.astype(BF16)
    return high, (a - high.astype(F32)).astype(BF16)


def mm3(a, b):
    bh, bl = split(b)
    wide = b.shape[1]
    pair = jnp.concatenate([bh, bl], 1)
    alone = jnp.concatenate([bh, jnp.zeros_like(bh)], 1)
    both = dot(jnp.concatenate(split(a), 1), jnp.concatenate([pair, alone], 0))
    return both[:, :wide] + both[:, wide:]


def after(earlier, later):
    return mm3(earlier, later[:HD]) + pad_top(later[HD:])


def pad_top(state):
    return jnp.concatenate([jnp.zeros((HD, HD), F32), state], 0)


def prepend(raw, acc):
    both = dot(raw, jnp.concatenate(split(acc[:HD]), 1))
    return both[:, :HD] + both[:, HD:] + pad_top(acc[HD:])


def twice(a, b):
    return dot(jnp.concatenate(split(a), 1), jnp.concatenate([b, b], 0))


def append(acc, raw):
    return twice(acc, raw[:HD]) + pad_top(raw[HD:].astype(F32))


def invert(lowers):
    row = lax.broadcasted_iota(jnp.int32, (CHUNK, CHUNK), 0)
    col = lax.broadcasted_iota(jnp.int32, (CHUNK, CHUNK), 1)

    def pick(low, bits):
        r, c = lax.shift_right_logical(row, bits), lax.shift_right_logical(col, bits)
        mask = (lax.bitwise_and(r, 1) == 1) & (c == r - 1)
        return jnp.where(mask, low, 0.0)

    eye = (row == col).astype(F32)
    inverses = [eye - pick(low, 0) for low in lowers]
    bits = 1
    while (1 << bits) < CHUNK:
        first = [mm3(x, pick(low, bits)) for x, low in zip(inverses, lowers)]
        inverses = [x - mm3(f, x) for x, f in zip(inverses, first)]
        bits += 1
    return inverses


def layer(
    x_chips, z_chips,
    tok, wq, wk, wv, wb_in, bias_in, conv_in, gain_in, wo,
    out,
    wb, bias, conv, gain,
    gathered, halo, weights, outw, padded, logits,
    q_eff, o_loc, ring, lines, left, right, own_f, prefix, duo, mate, next_state, state, entering,
    give, got,
    load_sem, tok_send, tok_recv, halo_send, halo_recv, w_send, w_recv,
    duo_send, duo_recv, ring_send, ring_recv, line_send, line_recv, give_send, got_recv,
):
    s, h = lax.axis_index("seq"), lax.axis_index("head")
    shards = x_chips * z_chips
    y, c = h // 2, h % 2
    x, z = s // z_chips, s % z_chips
    up, down, far = (y + 1) % Y_CHIPS, (y + 3) % Y_CHIPS, (y + 2) % Y_CHIPS
    other = 1 - c

    def head_of(yy, cc):
        return yy * 2 + cc

    partner = (s, head_of(y, other))

    def remote(src, dst, send, recv, device):
        return pltpu.make_async_remote_copy(
            src_ref=src, dst_ref=dst, send_sem=send, recv_sem=recv,
            device_id=device, device_id_type=MESH,
        )

    def arrived(dst, recv):
        remote(dst, dst, recv, recv, partner).wait_recv()

    def settle(shape_of, sem):
        pltpu.make_async_copy(shape_of, shape_of, sem).wait()

    loads = [
        pltpu.make_async_copy(w, weights.at[:, pl.ds(i * HD, HD)], load_sem.at[0])
        for i, w in enumerate((wq, wk, wv))
    ]
    own_wo = pltpu.make_async_copy(wo, outw.at[h], load_sem.at[1])
    small = [
        pltpu.make_async_copy(src, dst, load_sem.at[3 + i])
        for i, (src, dst) in enumerate(
            ((wb_in, wb), (bias_in, bias), (conv_in, conv), (gain_in, gain))
        )
    ]
    own_tok = [
        pltpu.make_async_copy(
            tok.at[pl.ds(i * PART, PART)], gathered.at[y, c, i], load_sem.at[2]
        )
        for i in range(4)
    ]
    for copy in (*own_tok, *small, *loads, own_wo):
        copy.start()

    barrier = pltpu.get_barrier_semaphore()

    def greet(device):
        pl.semaphore_signal(barrier, inc=1, device_id=device, device_id_type=MESH)

    for step in range(1, 8):
        greet((s, (h + step) % 8))
    odd = z % 2
    greet((x * z_chips + z + 1 - 2 * odd, h))
    offsets = (2, 4) if z_chips == 16 else (2,)

    @pl.when(odd == 0)
    def _():
        for offset in offsets:
            greet((x * z_chips + (z + offset) % z_chips, h))
            greet((x * z_chips + (z + z_chips - offset) % z_chips, h))
        for step in range(1, x_chips):
            greet((((x + step) % x_chips) * z_chips + z, h))

    @pl.when(s > 0)
    def _():
        greet((s - 1, 7))

    sends_halo = (h == 7) & (s < shards - 1)

    @pl.when(sends_halo)
    def _():
        for peer in range(8):
            greet((s + 1, peer))

    pl.semaphore_wait(
        barrier,
        8 + jnp.where(odd == 0, 2 * len(offsets) + x_chips - 1, 0) + jnp.where(s > 0, 1, 0) + jnp.where(sends_halo, 8, 0),
    )

    def tok_copy(src, yy, cc, part, device, kind):
        recv = tok_recv.at[yy, 4] if device is partner else tok_recv.at[yy, part]
        remote(src, gathered.at[yy, cc, part], tok_send.at[kind], recv, device).start()

    def relay(yy, half, device):
        tok_copy(gathered.at[yy, c, half], yy, c, half, device, 1)

    to_up, to_down = (s, head_of(up, c)), (s, head_of(down, c))
    settle(gathered.at[y, c], load_sem.at[2])
    own = [gathered.at[y, c, i] for i in range(4)]
    for first, second in ((0, 2), (1, 3), (2, 0), (3, 1)):
        tok_copy(own[first], y, c, first, to_up, 0)
        tok_copy(own[second], y, c, second, to_down, 0)
    for i in range(4):
        tok_copy(own[i], y, c, i, partner, 0)

    def halo_copy(peer):
        return remote(
            tok.at[pl.ds(ROWS - HALO, HALO)], halo, halo_send, halo_recv, (s + 1, peer)
        )

    @pl.when(sends_halo)
    def _():
        for peer in range(8):
            halo_copy(peer).start()

    @pl.when(s == 0)
    def _():
        halo[...] = jnp.zeros_like(halo)

    for copy in small:
        copy.wait()
    rate_rows = jnp.broadcast_to(wb[...].astype(F32), (HD, D))
    weights[:, pl.ds(3 * HD, HD)] = jnp.transpose(rate_rows).astype(BF16)
    settle(weights.at[:, pl.ds(0, 3 * HD)], load_sem.at[0])

    def project(yy):
        block = gathered[yy].reshape(CHUNK, D)
        result = dot(block, weights[...])
        start = pl.multiple_of(yy * CHUNK, CHUNK)
        padded[pl.ds(start + HALO, CHUNK), :] = result[:, : 3 * HD].astype(BF16).astype(F32)
        logits[pl.ds(start, CHUNK), :] = result[:, 3 * HD :]

    def tok_arrived(yy, part):
        arrived(gathered.at[yy, c, part], tok_recv.at[yy, part])

    def tok_other_arrived(yy):
        arrived(gathered.at[yy, other], tok_recv.at[yy, 4])

    def near_arrived(up_part, down_part, onward):
        tok_arrived(down, up_part)
        if onward:
            relay(down, up_part, to_up)
        relay(down, up_part, partner)
        tok_arrived(up, down_part)
        if onward:
            relay(up, down_part, to_down)
        relay(up, down_part, partner)

    near_arrived(0, 2, True)
    near_arrived(1, 3, True)
    tok_other_arrived(y)
    project(y)
    near_arrived(2, 0, False)
    near_arrived(3, 1, False)
    @pl.when(s > 0)
    def _():
        arrived(halo, halo_recv)

    edge = dot(halo[...], weights[...])[:, : 3 * HD].astype(BF16).astype(F32)
    padded[pl.ds(0, HALO), :] = edge
    for part in (0, 2, 1, 3):
        tok_arrived(far, part)
        relay(far, part, partner)
    for yy in (down, up):
        tok_other_arrived(yy)
        project(yy)
    tok_other_arrived(far)
    project(far)

    own_wo.wait()

    def wo_copy(src, slot, half, device):
        rows = pl.ds(half * ROWS, ROWS)
        recv = w_recv.at[slot // 2, 2 if device is partner else half]
        remote(src.at[rows], outw.at[slot, rows], w_send, recv, device).start()

    def wo_relay(yy, half, device):
        slot = head_of(yy, c)
        wo_copy(outw.at[slot], slot, half, device)

    def wo_arrived(yy, half):
        slot = head_of(yy, c)
        arrived(outw.at[slot, pl.ds(half * ROWS, ROWS)], w_recv.at[yy, half])

    wo_copy(outw.at[h], h, 0, to_up)
    wo_copy(outw.at[h], h, 1, to_down)
    wo_copy(outw.at[h], h, 1, to_up)
    wo_copy(outw.at[h], h, 0, to_down)
    wo_copy(outw.at[h], h, 0, partner)
    wo_copy(outw.at[h], h, 1, partner)

    def wo_relay_near():
        for yy, first, onward in ((down, 0, to_up), (up, 1, to_down)):
            wo_arrived(yy, first)
            wo_relay(yy, first, onward)
        for yy in (down, up):
            for half in range(2):
                if (yy is down) == (half == 1):
                    wo_arrived(yy, half)
                wo_relay(yy, half, partner)

    def wo_relay_far():
        for half in range(2):
            wo_arrived(far, half)
            wo_relay(far, half, partner)

    row = lax.broadcasted_iota(jnp.int32, (CHUNK, CHUNK), 0)
    col = lax.broadcasted_iota(jnp.int32, (CHUNK, CHUNK), 1)
    parts, lowers, rights, attends = [], [], [], []
    for n in range(CHUNKS):
        base = n * CHUNK
        acts = []
        for i in range(3):
            lanes = pl.ds(i * HD, HD)
            total = padded[pl.ds(base + HALO - 3, CHUNK), lanes] * conv[i, 0:1]
            for j in range(1, 4):
                total = total + padded[pl.ds(base + HALO - 3 + j, CHUNK), lanes] * conv[i, j : j + 1]
            acts.append((total / (1.0 + jnp.exp(-total))).astype(BF16))
        query, key, value = acts
        key32 = key.astype(F32)
        inv = 1.0 / jnp.sqrt(jnp.sum(key32 * key32, -1, keepdims=True) + 1e-06)
        beta = 2.0 * jax.nn.sigmoid(logits[pl.ds(base, CHUNK), :] + bias[0])
        rate = beta * inv
        gram = dot(key, key, NT)
        lowers.append(jnp.where(row > col, (rate * inv) * gram, 0.0))
        rights.append(
            jnp.concatenate([(rate * inv) * key32, rate * value.astype(F32)], 1)
        )
        attends.append(jnp.where(row >= col, dot(query, key, NT), 0.0).astype(BF16))
        parts.append((query, key))
    inverses = invert(lowers)
    eye = (row == col).astype(F32)
    lead = jnp.concatenate([eye, jnp.zeros((HD, HD), F32)], 0)
    before, entry, reached = lead, [], []
    for n in range(CHUNKS):
        query, key = parts[n]
        solved = mm3(inverses[n], rights[n])
        high, low = split(solved)
        moved = dot(jnp.concatenate([high, low], 0), jnp.concatenate([key, key], 0), TN)
        step = jnp.concatenate([eye - moved[:HD], moved[HD:]], 0)
        entry.append(before)
        reached.append(high)
        before = step if n == 0 else after(before, step)

    def finish_outputs():
        for n in range(CHUNKS):
            reach = dot(attends[n], reached[n])
            eff = (parts[n][0].astype(F32) - reach[:, :HD]).astype(BF16)
            if n == 0:
                q_eff[pl.ds(0, CHUNK), :] = eff
                o_loc[pl.ds(0, CHUNK), :] = reach[:, HD:]
            else:
                turned = dot(eff, entry[n].astype(BF16), NT)
                q_eff[pl.ds(n * CHUNK, CHUNK), :] = turned[:, :HD].astype(BF16)
                o_loc[pl.ds(n * CHUNK, CHUNK), :] = turned[:, HD:] + reach[:, HD:]


    pairs = z_chips // 2
    j = z // 2

    def at_z(offset):
        return (x * z_chips + (z + z_chips + offset) % z_chips, h)

    duo[...] = before.astype(BF16)
    to_even = remote(duo, mate, duo_send.at[0], duo_recv.at[0], at_z(-1))
    to_odd = remote(next_state, next_state, duo_send.at[1], duo_recv.at[1], at_z(1))

    @pl.when(odd == 1)
    def _():
        to_even.start()

    finish_outputs()

    def ring_copy(slot, q, offset, sem):
        remote(
            ring.at[slot, q], ring.at[slot, q], ring_send, ring_recv.at[slot, sem],
            at_z(2 * offset),
        ).start()

    def compose(k):
        slot = (j + pairs - k) % pairs
        side = jnp.where(k > j, 1, 0)
        left[side] = prepend(ring[slot].reshape(2 * HD, HD), left[side])
        if 2 * k < pairs:
            slot_r = (j + k) % pairs
            side_r = jnp.where(j + k >= pairs, 1, 0)
            right[side_r] = append(right[side_r], ring[slot_r].reshape(2 * HD, HD))

    def ring_arrived(k):
        if 2 * k < pairs:
            for slot in ((j + pairs - k) % pairs, (j + k) % pairs):
                arrived(ring.at[slot], ring_recv.at[slot, 0])
        else:
            slot = (j + k) % pairs
            for side in range(2):
                arrived(ring.at[slot, pl.ds(side * HALF_SUBS, HALF_SUBS)], ring_recv.at[slot, side])

    def scan_pairs():
        for i in range(2):
            left[i] = lead
            right[i] = lead
        arrived(mate, duo_recv.at[0])
        own_f[...] = append(before, mate[...])
        ring[j] = own_f[...].astype(BF16).reshape(SUBS, 2 * HD // SUBS, HD)
        if pairs == 8:
            for q in range(SUBS):
                ring_copy(j, q, 2, q)
                ring_copy(j, q, -2, q)
            for q in range(SUBS):
                ring_copy(j, q, 1, 0)
                ring_copy(j, q, -1, 0)
            back, ahead = (j + pairs - 2) % pairs, (j + 2) % pairs
            for q in range(SUBS):
                arrived(ring.at[back, q], ring_recv.at[back, q])
                if q < HALF_SUBS:
                    ring_copy(back, q, 2, 0)
                ring_copy(back, q, 1, 0)
                arrived(ring.at[ahead, q], ring_recv.at[ahead, q])
                if q >= HALF_SUBS:
                    ring_copy(ahead, q, -2, 1)
                ring_copy(ahead, q, -1, 0)
            wo_relay_near()
            ring_arrived(1)
            compose(1)
            compose(2)
            wo_relay_far()
            ring_arrived(3)
            compose(3)
        else:
            for q in range(SUBS):
                ring_copy(j, q, 1 if q < HALF_SUBS else -1, q // HALF_SUBS)
            wo_relay_near()
            wo_relay_far()
        ring_arrived(pairs // 2)
        compose(pairs // 2)
        prefix[...] = after(right[1], left[0])
        line = after(prefix[...], after(own_f[...], after(right[0], left[1])))

        lines[x] = line.astype(BF16).reshape(2, HD, HD)
        moves = [
            (0, 2, 1), (0, 1, 1), (0, 3, 1), (1, 3, 0), (1, 3, 1),
            (1, 2, 0), (1, 2, 1), (2, 3, 0), (2, 3, 1),
        ]

        def line_copy(i):
            slot, to, part = moves[i]
            return remote(
                lines.at[slot, part], lines.at[slot, part], line_send,
                line_recv.at[slot, part], (to * z_chips + z, h),
            )

        def line_arrived(slot, part):
            arrived(lines.at[slot, part], line_recv.at[slot, part])

        if x_chips == 4:
            for i, move in enumerate(moves):

                @pl.when(x == move[0])
                def _():
                    line_copy(i).start()

        entering[...] = jnp.zeros_like(entering)
        for k in range(x_chips - 1):

            @pl.when(k < x)
            def _():
                line_arrived(k, 1)
                if k == 0:
                    entering[...] = lines[0, 1].astype(F32)
                else:
                    line_arrived(k, 0)
                    entering[...] = twice(entering[...], lines[k, 0]) + lines[k, 1].astype(F32)

        own_in = mm3(entering[...], prefix[pl.ds(0, HD)]) + prefix[pl.ds(HD, HD)]
        next_state[...] = (mm3(own_in, before[:HD]) + before[HD:]).astype(BF16)
        to_odd.start()
        state[...] = own_in

    @pl.when(odd == 0)
    def _():
        scan_pairs()

    @pl.when(odd == 1)
    def _():
        wo_relay_near()
        wo_relay_far()
        arrived(next_state, duo_recv.at[1])
        state[...] = next_state[...].astype(F32)

    terms = jnp.concatenate(split(state[...]), 0)
    both = dot(q_eff[...], terms, NT)
    outputs = both[:, :HD] + both[:, HD:] + o_loc[...]
    scale = lax.rsqrt(jnp.mean(outputs * outputs, -1, keepdims=True) + 1e-05)
    give[...] = (outputs * scale * gain[...]).astype(BF16).reshape(Y_CHIPS, 2, ROWS, HD)
    for yy, cc in (
        (far, c), (far, other), (up, c), (down, c), (up, other), (down, other), (y, other)
    ):
        remote(
            give.at[yy, cc], got.at[h], give_send, got_recv.at[h], (s, head_of(yy, cc))
        ).start()
    got[h] = give[y, c]
    for yy in (y, up, down, far):
        arrived(outw.at[head_of(yy, other)], w_recv.at[yy, 2])
    mixed = dot(got[h], outw[h]).astype(BF16).astype(F32)
    for peer in (
        head_of(y, other), head_of(up, c), head_of(down, c), head_of(up, other),
        head_of(down, other), head_of(far, c), head_of(far, other),
    ):
        arrived(got.at[peer], got_recv.at[peer])
        mixed = mixed + dot(got[peer], outw[peer]).astype(BF16).astype(F32)
    out[...] = mixed.astype(BF16)

    settle(gathered.at[pl.ds(0, 3), 0], tok_send.at[0])
    settle(gathered.at[:, 0], tok_send.at[1])
    settle(outw.at[pl.ds(0, 7)], w_send)
    settle(got.at[pl.ds(0, 7)], give_send)

    @pl.when(odd == 1)
    def _():
        to_even.wait_send()

    @pl.when(odd == 0)
    def _():
        to_odd.wait_send()
        settle(ring.at[pl.ds(0, RING_SENDS[pairs])], ring_send)

    if x_chips == 4:
        for line_x, count in enumerate((3, 4, 2)):

            @pl.when((odd == 0) & (x == line_x))
            def _():
                settle(lines.at[pl.ds(0, count), 0], line_send)

    @pl.when(sends_halo)
    def _():
        settle(gathered.at[0, 0], halo_send)


def local(x_chips, z_chips, tokens, w_query, w_key, w_value, w_beta, beta_bias, conv_weight, norm_gain, w_out):
    hbm = pl.BlockSpec(memory_space=pltpu.HBM)
    vmem = pl.BlockSpec(memory_space=pltpu.VMEM)
    dma = pltpu.SemaphoreType.DMA
    return pl.pallas_call(
        functools.partial(layer, x_chips, z_chips),
        out_shape=jax.ShapeDtypeStruct((ROWS, D), BF16),
        in_specs=[hbm] * 9,
        out_specs=vmem,
        scratch_shapes=[
            pltpu.VMEM((1, D), BF16),
            pltpu.SMEM((1,), F32),
            pltpu.VMEM((3, 4, HD), F32),
            pltpu.VMEM((1, HD), F32),
            pltpu.VMEM((Y_CHIPS, 2, 4, PART, D), BF16),
            pltpu.VMEM((HALO, D), BF16),
            pltpu.VMEM((D, 4 * HD), BF16),
            pltpu.VMEM((8, HD, D), BF16),
            pltpu.VMEM((HALO + SHARD, 3 * HD), F32),
            pltpu.VMEM((SHARD, HD), F32),
            pltpu.VMEM((SHARD, HD), BF16),
            pltpu.VMEM((SHARD, HD), F32),
            pltpu.VMEM((z_chips // 2, SUBS, 2 * HD // SUBS, HD), BF16),
            pltpu.VMEM((x_chips, 2, HD, HD), BF16),
            pltpu.VMEM((2, 2 * HD, HD), F32),
            pltpu.VMEM((2, 2 * HD, HD), F32),
            pltpu.VMEM((2 * HD, HD), F32),
            pltpu.VMEM((2 * HD, HD), F32),
            pltpu.VMEM((2 * HD, HD), BF16),
            pltpu.VMEM((2 * HD, HD), BF16),
            pltpu.VMEM((HD, HD), BF16),
            pltpu.VMEM((HD, HD), F32),
            pltpu.VMEM((HD, HD), F32),
            pltpu.VMEM((Y_CHIPS, 2, ROWS, HD), BF16),
            pltpu.VMEM((8, ROWS, HD), BF16),
            dma((7,)),
            dma((2,)),
            dma((Y_CHIPS, 5)),
            dma,
            dma,
            dma,
            dma((Y_CHIPS, 3)),
            dma((2,)),
            dma((2,)),
            dma,
            dma((z_chips // 2, SUBS)),
            dma,
            dma((x_chips, 2)),
            dma,
            dma((8,)),
        ],
        compiler_params=pltpu.CompilerParams(
            collective_id=0, has_side_effects=True, vmem_limit_bytes=48 * 1024 * 1024
        ),
    )(
        keep(tokens), keep(w_query), keep(w_key), keep(w_value),
        keep(w_beta.reshape(1, D)), beta_bias, keep(conv_weight),
        keep(norm_gain.reshape(1, HD)), keep(w_out),
    )


def keep(a):
    return pltpu.with_memory_space_constraint(a, pltpu.HBM)


def solution(mesh):
    z_chips = Z_CHIPS
    x_chips = mesh.shape["seq"] // z_chips
    in_specs = (
        P(("seq", "head"), None),
        P(None, "head"),
        P(None, "head"),
        P(None, "head"),
        P(None, "head"),
        P("head"),
        P(None, None, "head"),
        P("head"),
        P("head", None),
    )
    out_specs = P(("seq", "head"), None)
    return jax.shard_map(
        functools.partial(local, x_chips, z_chips),
        mesh=mesh, in_specs=in_specs, out_specs=out_specs, check_vma=False,
    )
```

```python
import functools

import jax
import jax.numpy as jnp
from jax import lax
from jax.experimental import pallas as pl
from jax.experimental.pallas import tpu as pltpu
from jax.sharding import PartitionSpec as P

F32, BF16 = jnp.float32, jnp.bfloat16
MESH = pl.DeviceIdType.MESH
Z_CHIPS = 16
Y_CHIPS = 4
D = 1024
HD = 128
ROWS = 64
SHARD = 512
CHUNK = 128
CHUNKS = SHARD // CHUNK
PART = 16
HALO = 8
SUBS = 4
HALF_SUBS = SUBS // 2
RING_SENDS = {2: 1, 8: 7}

NN = (((1,), (0,)), ((), ()))
NT = (((1,), (1,)), ((), ()))
TN = (((0,), (0,)), ((), ()))


def dot(a, b, dims=NN):
    return lax.dot_general(a, b, dims, preferred_element_type=F32)


def split(a):
    high = a.astype(BF16)
    return high, (a - high.astype(F32)).astype(BF16)


def mm3(a, b):
    bh, bl = split(b)
    wide = b.shape[1]
    pair = jnp.concatenate([bh, bl], 1)
    alone = jnp.concatenate([bh, jnp.zeros_like(bh)], 1)
    both = dot(jnp.concatenate(split(a), 1), jnp.concatenate([pair, alone], 0))
    return both[:, :wide] + both[:, wide:]


def after(earlier, later):
    return mm3(earlier, later[:HD]) + pad_top(later[HD:])


def pad_top(state):
    return jnp.concatenate([jnp.zeros((HD, HD), F32), state], 0)


def prepend(raw, acc):
    both = dot(raw, jnp.concatenate(split(acc[:HD]), 1))
    return both[:, :HD] + both[:, HD:] + pad_top(acc[HD:])


def twice(a, b):
    return dot(jnp.concatenate(split(a), 1), jnp.concatenate([b, b], 0))


def append(acc, raw):
    return twice(acc, raw[:HD]) + pad_top(raw[HD:].astype(F32))


def invert(lowers):
    row = lax.broadcasted_iota(jnp.int32, (CHUNK, CHUNK), 0)
    col = lax.broadcasted_iota(jnp.int32, (CHUNK, CHUNK), 1)

    def pick(low, bits):
        r, c = lax.shift_right_logical(row, bits), lax.shift_right_logical(col, bits)
        mask = (lax.bitwise_and(r, 1) == 1) & (c == r - 1)
        return jnp.where(mask, low, 0.0)

    eye = (row == col).astype(F32)
    inverses = [eye - pick(low, 0) for low in lowers]
    bits = 1
    while (1 << bits) < CHUNK:
        first = [mm3(x, pick(low, bits)) for x, low in zip(inverses, lowers)]
        inverses = [x - mm3(f, x) for x, f in zip(inverses, first)]
        bits += 1
    return inverses


def layer(
    x_chips, z_chips,
    tok, wq, wk, wv, wb_in, bias_in, conv_in, gain_in, wo,
    out,
    wb, bias, conv, gain,
    gathered, halo, weights, outw, padded, logits,
    q_eff, o_loc, ring, lines, left, right, own_f, prefix, duo, mate, next_state, state, entering,
    give, got,
    load_sem, tok_send, tok_recv, halo_send, halo_recv, w_send, w_recv,
    duo_send, duo_recv, ring_send, ring_recv, line_send, line_recv, give_send, got_recv,
):
    s, h = lax.axis_index("seq"), lax.axis_index("head")
    shards = x_chips * z_chips
    y, c = h // 2, h % 2
    x, z = s // z_chips, s % z_chips
    up, down, far = (y + 1) % Y_CHIPS, (y + 3) % Y_CHIPS, (y + 2) % Y_CHIPS
    other = 1 - c

    def head_of(yy, cc):
        return yy * 2 + cc

    partner = (s, head_of(y, other))

    def remote(src, dst, send, recv, device):
        return pltpu.make_async_remote_copy(
            src_ref=src, dst_ref=dst, send_sem=send, recv_sem=recv,
            device_id=device, device_id_type=MESH,
        )

    def arrived(dst, recv):
        remote(dst, dst, recv, recv, partner).wait_recv()

    def settle(shape_of, sem):
        pltpu.make_async_copy(shape_of, shape_of, sem).wait()

    loads = [
        pltpu.make_async_copy(w, weights.at[:, pl.ds(i * HD, HD)], load_sem.at[0])
        for i, w in enumerate((wq, wk, wv))
    ]
    own_wo = pltpu.make_async_copy(wo, outw.at[h], load_sem.at[1])
    small = [
        pltpu.make_async_copy(src, dst, load_sem.at[3 + i])
        for i, (src, dst) in enumerate(
            ((wb_in, wb), (bias_in, bias), (conv_in, conv), (gain_in, gain))
        )
    ]
    own_tok = [
        pltpu.make_async_copy(
            tok.at[pl.ds(i * PART, PART)], gathered.at[y, c, i], load_sem.at[2]
        )
        for i in range(4)
    ]
    for copy in (*own_tok, *small, *loads, own_wo):
        copy.start()

    barrier = pltpu.get_barrier_semaphore()

    def greet(device):
        pl.semaphore_signal(barrier, inc=1, device_id=device, device_id_type=MESH)

    for step in range(1, 8):
        greet((s, (h + step) % 8))
    odd = z % 2
    greet((x * z_chips + z + 1 - 2 * odd, h))
    offsets = (2, 4) if z_chips == 16 else (2,)

    @pl.when(odd == 0)
    def _():
        for offset in offsets:
            greet((x * z_chips + (z + offset) % z_chips, h))
            greet((x * z_chips + (z + z_chips - offset) % z_chips, h))
        for step in range(1, x_chips):
            greet((((x + step) % x_chips) * z_chips + z, h))

    @pl.when(s > 0)
    def _():
        greet((s - 1, 7))

    sends_halo = (h == 7) & (s < shards - 1)

    @pl.when(sends_halo)
    def _():
        for peer in range(8):
            greet((s + 1, peer))

    pl.semaphore_wait(
        barrier,
        8 + jnp.where(odd == 0, 2 * len(offsets) + x_chips - 1, 0) + jnp.where(s > 0, 1, 0) + jnp.where(sends_halo, 8, 0),
    )

    def tok_copy(src, yy, cc, part, device, kind):
        recv = tok_recv.at[yy, 4] if device is partner else tok_recv.at[yy, part]
        remote(src, gathered.at[yy, cc, part], tok_send.at[kind], recv, device).start()

    def relay(yy, half, device):
        tok_copy(gathered.at[yy, c, half], yy, c, half, device, 1)

    to_up, to_down = (s, head_of(up, c)), (s, head_of(down, c))
    settle(gathered.at[y, c], load_sem.at[2])
    own = [gathered.at[y, c, i] for i in range(4)]
    for first, second in ((0, 2), (1, 3), (2, 0), (3, 1)):
        tok_copy(own[first], y, c, first, to_up, 0)
        tok_copy(own[second], y, c, second, to_down, 0)
    for i in range(4):
        tok_copy(own[i], y, c, i, partner, 0)

    def halo_copy(peer):
        return remote(
            tok.at[pl.ds(ROWS - HALO, HALO)], halo, halo_send, halo_recv, (s + 1, peer)
        )

    @pl.when(sends_halo)
    def _():
        for peer in range(8):
            halo_copy(peer).start()

    @pl.when(s == 0)
    def _():
        halo[...] = jnp.zeros_like(halo)

    for copy in small:
        copy.wait()
    rate_rows = jnp.broadcast_to(wb[...].astype(F32), (HD, D))
    weights[:, pl.ds(3 * HD, HD)] = jnp.transpose(rate_rows).astype(BF16)
    settle(weights.at[:, pl.ds(0, 3 * HD)], load_sem.at[0])

    def project(yy):
        block = gathered[yy].reshape(CHUNK, D)
        result = dot(block, weights[...])
        start = pl.multiple_of(yy * CHUNK, CHUNK)
        padded[pl.ds(start + HALO, CHUNK), :] = result[:, : 3 * HD].astype(BF16).astype(F32)
        logits[pl.ds(start, CHUNK), :] = result[:, 3 * HD :]

    def tok_arrived(yy, part):
        arrived(gathered.at[yy, c, part], tok_recv.at[yy, part])

    def tok_other_arrived(yy):
        arrived(gathered.at[yy, other], tok_recv.at[yy, 4])

    def near_arrived(up_part, down_part, onward):
        tok_arrived(down, up_part)
        if onward:
            relay(down, up_part, to_up)
        relay(down, up_part, partner)
        tok_arrived(up, down_part)
        if onward:
            relay(up, down_part, to_down)
        relay(up, down_part, partner)

    near_arrived(0, 2, True)
    near_arrived(1, 3, True)
    tok_other_arrived(y)
    project(y)
    near_arrived(2, 0, False)
    near_arrived(3, 1, False)
    @pl.when(s > 0)
    def _():
        arrived(halo, halo_recv)

    edge = dot(halo[...], weights[...])[:, : 3 * HD].astype(BF16).astype(F32)
    padded[pl.ds(0, HALO), :] = edge
    for part in (0, 2, 1, 3):
        tok_arrived(far, part)
        relay(far, part, partner)
    for yy in (down, up):
        tok_other_arrived(yy)
        project(yy)
    tok_other_arrived(far)
    project(far)

    own_wo.wait()

    def wo_copy(src, slot, half, device):
        rows = pl.ds(half * ROWS, ROWS)
        recv = w_recv.at[slot // 2, 2 if device is partner else half]
        remote(src.at[rows], outw.at[slot, rows], w_send, recv, device).start()

    def wo_relay(yy, half, device):
        slot = head_of(yy, c)
        wo_copy(outw.at[slot], slot, half, device)

    def wo_arrived(yy, half):
        slot = head_of(yy, c)
        arrived(outw.at[slot, pl.ds(half * ROWS, ROWS)], w_recv.at[yy, half])

    wo_copy(outw.at[h], h, 0, to_up)
    wo_copy(outw.at[h], h, 1, to_down)
    wo_copy(outw.at[h], h, 1, to_up)
    wo_copy(outw.at[h], h, 0, to_down)
    wo_copy(outw.at[h], h, 0, partner)
    wo_copy(outw.at[h], h, 1, partner)

    def wo_relay_near():
        for yy, first, onward in ((down, 0, to_up), (up, 1, to_down)):
            wo_arrived(yy, first)
            wo_relay(yy, first, onward)
        for yy in (down, up):
            for half in range(2):
                if (yy is down) == (half == 1):
                    wo_arrived(yy, half)
                wo_relay(yy, half, partner)

    def wo_relay_far():
        for half in range(2):
            wo_arrived(far, half)
            wo_relay(far, half, partner)

    row = lax.broadcasted_iota(jnp.int32, (CHUNK, CHUNK), 0)
    col = lax.broadcasted_iota(jnp.int32, (CHUNK, CHUNK), 1)
    parts, lowers, rights, attends = [], [], [], []
    for n in range(CHUNKS):
        base = n * CHUNK
        acts = []
        for i in range(3):
            lanes = pl.ds(i * HD, HD)
            total = padded[pl.ds(base + HALO - 3, CHUNK), lanes] * conv[i, 0:1]
            for j in range(1, 4):
                total = total + padded[pl.ds(base + HALO - 3 + j, CHUNK), lanes] * conv[i, j : j + 1]
            acts.append((total / (1.0 + jnp.exp(-total))).astype(BF16))
        query, key, value = acts
        key32 = key.astype(F32)
        inv = 1.0 / jnp.sqrt(jnp.sum(key32 * key32, -1, keepdims=True) + 1e-06)
        beta = 2.0 * jax.nn.sigmoid(logits[pl.ds(base, CHUNK), :] + bias[0])
        rate = beta * inv
        gram = dot(key, key, NT)
        lowers.append(jnp.where(row > col, (rate * inv) * gram, 0.0))
        rights.append(
            jnp.concatenate([(rate * inv) * key32, rate * value.astype(F32)], 1)
        )
        attends.append(jnp.where(row >= col, dot(query, key, NT), 0.0).astype(BF16))
        parts.append((query, key))
    inverses = invert(lowers)
    eye = (row == col).astype(F32)
    lead = jnp.concatenate([eye, jnp.zeros((HD, HD), F32)], 0)
    before, entry, reached = lead, [], []
    for n in range(CHUNKS):
        query, key = parts[n]
        solved = mm3(inverses[n], rights[n])
        high, low = split(solved)
        moved = dot(jnp.concatenate([high, low], 0), jnp.concatenate([key, key], 0), TN)
        step = jnp.concatenate([eye - moved[:HD], moved[HD:]], 0)
        entry.append(before)
        reached.append(high)
        before = step if n == 0 else after(before, step)

    def finish_outputs():
        for n in range(CHUNKS):
            reach = dot(attends[n], reached[n])
            eff = (parts[n][0].astype(F32) - reach[:, :HD]).astype(BF16)
            if n == 0:
                q_eff[pl.ds(0, CHUNK), :] = eff
                o_loc[pl.ds(0, CHUNK), :] = reach[:, HD:]
            else:
                turned = dot(eff, entry[n].astype(BF16), NT)
                q_eff[pl.ds(n * CHUNK, CHUNK), :] = turned[:, :HD].astype(BF16)
                o_loc[pl.ds(n * CHUNK, CHUNK), :] = turned[:, HD:] + reach[:, HD:]


    pairs = z_chips // 2
    j = z // 2

    def at_z(offset):
        return (x * z_chips + (z + z_chips + offset) % z_chips, h)

    duo[...] = before.astype(BF16)
    tops, bottoms = pl.ds(0, HD), pl.ds(HD, HD)
    to_even = [
        remote(duo.at[rows], mate.at[rows], duo_send.at[0], duo_recv.at[2 * i], at_z(-1))
        for i, rows in enumerate((tops, bottoms))
    ]
    to_odd = remote(next_state, next_state, duo_send.at[1], duo_recv.at[1], at_z(1))

    @pl.when(odd == 1)
    def _():
        for copy in to_even:
            copy.start()

    finish_outputs()

    def ring_copy(slot, q, offset, sem):
        remote(
            ring.at[slot, q], ring.at[slot, q], ring_send, ring_recv.at[slot, sem],
            at_z(2 * offset),
        ).start()

    def compose(k):
        slot = (j + pairs - k) % pairs
        side = jnp.where(k > j, 1, 0)
        left[side] = prepend(ring[slot].reshape(2 * HD, HD), left[side])
        if 2 * k < pairs:
            slot_r = (j + k) % pairs
            side_r = jnp.where(j + k >= pairs, 1, 0)
            right[side_r] = append(right[side_r], ring[slot_r].reshape(2 * HD, HD))

    def ring_arrived(k):
        if 2 * k < pairs:
            for slot in ((j + pairs - k) % pairs, (j + k) % pairs):
                arrived(ring.at[slot], ring_recv.at[slot, 0])
        else:
            slot = (j + k) % pairs
            for side in range(2):
                arrived(ring.at[slot, pl.ds(side * HALF_SUBS, HALF_SUBS)], ring_recv.at[slot, side])

    def scan_pairs():
        for i in range(2):
            left[i] = lead
            right[i] = lead
        arrived(mate.at[tops], duo_recv.at[0])
        product = twice(before, mate[tops])
        own_f[tops] = product[:HD]
        ring[j, pl.ds(0, HALF_SUBS)] = product[:HD].astype(BF16).reshape(HALF_SUBS, 2 * HD // SUBS, HD)
        if pairs == 8:
            for q in range(HALF_SUBS):
                ring_copy(j, q, 2, q)
                ring_copy(j, q, -2, q)
        arrived(mate.at[bottoms], duo_recv.at[2])
        own_f[bottoms] = product[HD:] + mate[bottoms].astype(F32)
        ring[j, pl.ds(HALF_SUBS, HALF_SUBS)] = own_f[bottoms].astype(BF16).reshape(
            HALF_SUBS, 2 * HD // SUBS, HD
        )
        if pairs == 8:
            for q in range(HALF_SUBS, SUBS):
                ring_copy(j, q, 2, q)
                ring_copy(j, q, -2, q)
            for q in range(SUBS):
                ring_copy(j, q, 1, 0)
                ring_copy(j, q, -1, 0)
            back, ahead = (j + pairs - 2) % pairs, (j + 2) % pairs
            for q in range(SUBS):
                arrived(ring.at[back, q], ring_recv.at[back, q])
                if q < HALF_SUBS:
                    ring_copy(back, q, 2, 0)
                ring_copy(back, q, 1, 0)
                arrived(ring.at[ahead, q], ring_recv.at[ahead, q])
                if q >= HALF_SUBS:
                    ring_copy(ahead, q, -2, 1)
                ring_copy(ahead, q, -1, 0)
            wo_relay_near()
            ring_arrived(1)
            compose(1)
            compose(2)
            wo_relay_far()
            ring_arrived(3)
            compose(3)
        else:
            for q in range(SUBS):
                ring_copy(j, q, 1 if q < HALF_SUBS else -1, q // HALF_SUBS)
            wo_relay_near()
            wo_relay_far()
        ring_arrived(pairs // 2)
        compose(pairs // 2)
        prefix[...] = after(right[1], left[0])
        line = after(prefix[...], after(own_f[...], after(right[0], left[1])))

        lines[x] = line.astype(BF16).reshape(2, HD, HD)
        moves = [
            (0, 2, 1), (0, 1, 1), (0, 3, 1), (1, 3, 0), (1, 3, 1),
            (1, 2, 0), (1, 2, 1), (2, 3, 0), (2, 3, 1),
        ]

        def line_copy(i):
            slot, to, part = moves[i]
            return remote(
                lines.at[slot, part], lines.at[slot, part], line_send,
                line_recv.at[slot, part], (to * z_chips + z, h),
            )

        def line_arrived(slot, part):
            arrived(lines.at[slot, part], line_recv.at[slot, part])

        if x_chips == 4:
            for i, move in enumerate(moves):

                @pl.when(x == move[0])
                def _():
                    line_copy(i).start()

        entering[...] = jnp.zeros_like(entering)
        for k in range(x_chips - 1):

            @pl.when(k < x)
            def _():
                line_arrived(k, 1)
                if k == 0:
                    entering[...] = lines[0, 1].astype(F32)
                else:
                    line_arrived(k, 0)
                    entering[...] = twice(entering[...], lines[k, 0]) + lines[k, 1].astype(F32)

        own_in = mm3(entering[...], prefix[pl.ds(0, HD)]) + prefix[pl.ds(HD, HD)]
        next_state[...] = (mm3(own_in, before[:HD]) + before[HD:]).astype(BF16)
        to_odd.start()
        state[...] = own_in

    @pl.when(odd == 0)
    def _():
        scan_pairs()

    @pl.when(odd == 1)
    def _():
        wo_relay_near()
        wo_relay_far()
        arrived(next_state, duo_recv.at[1])
        state[...] = next_state[...].astype(F32)

    terms = jnp.concatenate(split(state[...]), 0)
    both = dot(q_eff[...], terms, NT)
    outputs = both[:, :HD] + both[:, HD:] + o_loc[...]
    scale = lax.rsqrt(jnp.mean(outputs * outputs, -1, keepdims=True) + 1e-05)
    give[...] = (outputs * scale * gain[...]).astype(BF16).reshape(Y_CHIPS, 2, ROWS, HD)
    for yy, cc in (
        (far, c), (far, other), (up, c), (down, c), (up, other), (down, other), (y, other)
    ):
        remote(
            give.at[yy, cc], got.at[h], give_send, got_recv.at[h], (s, head_of(yy, cc))
        ).start()
    got[h] = give[y, c]
    for yy in (y, up, down, far):
        arrived(outw.at[head_of(yy, other)], w_recv.at[yy, 2])
    mixed = dot(got[h], outw[h]).astype(BF16).astype(F32)
    for peer in (
        head_of(y, other), head_of(up, c), head_of(down, c), head_of(up, other),
        head_of(down, other), head_of(far, c), head_of(far, other),
    ):
        arrived(got.at[peer], got_recv.at[peer])
        mixed = mixed + dot(got[peer], outw[peer]).astype(BF16).astype(F32)
    out[...] = mixed.astype(BF16)

    settle(gathered.at[pl.ds(0, 3), 0], tok_send.at[0])
    settle(gathered.at[:, 0], tok_send.at[1])
    settle(outw.at[pl.ds(0, 7)], w_send)
    settle(got.at[pl.ds(0, 7)], give_send)

    @pl.when(odd == 1)
    def _():
        settle(duo, duo_send.at[0])

    @pl.when(odd == 0)
    def _():
        to_odd.wait_send()
        settle(ring.at[pl.ds(0, RING_SENDS[pairs])], ring_send)

    if x_chips == 4:
        for line_x, count in enumerate((3, 4, 2)):

            @pl.when((odd == 0) & (x == line_x))
            def _():
                settle(lines.at[pl.ds(0, count), 0], line_send)

    @pl.when(sends_halo)
    def _():
        settle(gathered.at[0, 0], halo_send)


def local(x_chips, z_chips, tokens, w_query, w_key, w_value, w_beta, beta_bias, conv_weight, norm_gain, w_out):
    hbm = pl.BlockSpec(memory_space=pltpu.HBM)
    vmem = pl.BlockSpec(memory_space=pltpu.VMEM)
    dma = pltpu.SemaphoreType.DMA
    return pl.pallas_call(
        functools.partial(layer, x_chips, z_chips),
        out_shape=jax.ShapeDtypeStruct((ROWS, D), BF16),
        in_specs=[hbm] * 9,
        out_specs=vmem,
        scratch_shapes=[
            pltpu.VMEM((1, D), BF16),
            pltpu.SMEM((1,), F32),
            pltpu.VMEM((3, 4, HD), F32),
            pltpu.VMEM((1, HD), F32),
            pltpu.VMEM((Y_CHIPS, 2, 4, PART, D), BF16),
            pltpu.VMEM((HALO, D), BF16),
            pltpu.VMEM((D, 4 * HD), BF16),
            pltpu.VMEM((8, HD, D), BF16),
            pltpu.VMEM((HALO + SHARD, 3 * HD), F32),
            pltpu.VMEM((SHARD, HD), F32),
            pltpu.VMEM((SHARD, HD), BF16),
            pltpu.VMEM((SHARD, HD), F32),
            pltpu.VMEM((z_chips // 2, SUBS, 2 * HD // SUBS, HD), BF16),
            pltpu.VMEM((x_chips, 2, HD, HD), BF16),
            pltpu.VMEM((2, 2 * HD, HD), F32),
            pltpu.VMEM((2, 2 * HD, HD), F32),
            pltpu.VMEM((2 * HD, HD), F32),
            pltpu.VMEM((2 * HD, HD), F32),
            pltpu.VMEM((2 * HD, HD), BF16),
            pltpu.VMEM((2 * HD, HD), BF16),
            pltpu.VMEM((HD, HD), BF16),
            pltpu.VMEM((HD, HD), F32),
            pltpu.VMEM((HD, HD), F32),
            pltpu.VMEM((Y_CHIPS, 2, ROWS, HD), BF16),
            pltpu.VMEM((8, ROWS, HD), BF16),
            dma((7,)),
            dma((2,)),
            dma((Y_CHIPS, 5)),
            dma,
            dma,
            dma,
            dma((Y_CHIPS, 3)),
            dma((2,)),
            dma((3,)),
            dma,
            dma((z_chips // 2, SUBS)),
            dma,
            dma((x_chips, 2)),
            dma,
            dma((8,)),
        ],
        compiler_params=pltpu.CompilerParams(
            collective_id=0, has_side_effects=True, vmem_limit_bytes=48 * 1024 * 1024
        ),
    )(
        keep(tokens), keep(w_query), keep(w_key), keep(w_value),
        keep(w_beta.reshape(1, D)), beta_bias, keep(conv_weight),
        keep(norm_gain.reshape(1, HD)), keep(w_out),
    )


def keep(a):
    return pltpu.with_memory_space_constraint(a, pltpu.HBM)


def solution(mesh):
    z_chips = Z_CHIPS
    x_chips = mesh.shape["seq"] // z_chips
    in_specs = (
        P(("seq", "head"), None),
        P(None, "head"),
        P(None, "head"),
        P(None, "head"),
        P(None, "head"),
        P("head"),
        P(None, None, "head"),
        P("head"),
        P("head", None),
    )
    out_specs = P(("seq", "head"), None)
    return jax.shard_map(
        functools.partial(local, x_chips, z_chips),
        mesh=mesh, in_specs=in_specs, out_specs=out_specs, check_vma=False,
    )
```
